256 devices in a mesh: phase: 8 (over y, core), seg: 32 (over z, x).
Axes of the slice: x: 4, y: 4, z: 8, core: 2. Of those that a mesh axis runs over, the one named last changes fastest.
Arguments:
- stream: bfloat16 [2, 4096, 4096], P(None, 'seg'), may hold values from -6 to 6
- doc_ids: int32 [2, 4096], P(None, 'seg'), may hold values from 0 to 7, never falling along the last dimension, each value on 1 to 2048 neighbouring positions
- in_proj: bfloat16 [8, 4096, 576], P('phase'), may hold values from -0.09375 to 0.09375
- conv_weight: float32 [8, 4, 4096], P('phase'), may hold values from -3 to 3
- conv_bias: float32 [8, 4096], P('phase'), may hold values from -3 to 3
- decay_log: float32 [8, 64], P('phase'), may hold values from -6.3 to 0.7
- step_bias: float32 [8, 64], P('phase'), may hold values from -4.5 to -2.5
- skip_gain: float32 [8, 64], P('phase'), may hold values from 0.5 to 1.5
- norm_gain: float32 [8, 4096], P('phase'), may hold values from 0.1 to 1.9
Outputs:
- layer_out: bfloat16 [8, 2, 4096, 4096], P('phase', None, 'seg')
The draws below stay inside these ranges and needn't reach their ends.
Inputs may be any that keep to these rules, and one draw needn't show every extreme that they name: `doc_ids`: ids never fall along a stream.
All inputs are finite; a program needn't handle non-finite values.
Results may differ from the reference program's by a relative error of at most 0.033.
Values may be sent and summed in bfloat16 or wider, within the bound.
A program may use at most 64 MiB of HBM per device.

```python
import math
import jax
import jax.numpy as jnp
import numpy as np
from jax import lax

HEADS = 64
HEAD_DIM = 64
STATE = 64
GROUPS = 4
KERNEL = 4
MICRO = 2
DOCS = 8
TOK_DEV = 128
CHANNELS = 4096
PROJ = 576
STREAM = 4096
LAYERS = 8


def draw_decay_log(key, part):
    subkeys = jax.random.split(key, 3)
    fast_share = 0.5
    fast_pick = jax.random.uniform(subkeys[0], (LAYERS, HEADS)) < fast_share
    slow_value = jax.random.uniform(subkeys[1], (LAYERS, HEADS), minval=math.log(0.002), maxval=math.log(0.012))
    fast_value = jax.random.uniform(subkeys[2], (LAYERS, HEADS), minval=math.log(0.5), maxval=math.log(2.0))
    return jnp.where(fast_pick, fast_value, slow_value).astype(jnp.float32)


def block_levels(stream_key, extent, cuts, smallest, largest):
    def one(axis_at, shards_of):
        heights = jax.random.uniform(jax.random.fold_in(jax.random.fold_in(stream_key, 6), axis_at), (shards_of,), jnp.float32, smallest / len(cuts), largest / len(cuts))
        return jnp.repeat(jnp.exp(heights), extent[axis_at] // shards_of).reshape((-1,) + (1,) * (len(extent) - axis_at - 1))

    level = one(*cuts[0])
    for cut in cuts[1:]:
        level = level * one(*cut)
    return level


def split_up(count, total, reach, skew):
    weights = [(1 << 20) // math.isqrt(standing ** skew) + 1 for standing in range(2, count + 1)]
    spare, counts = total - reach - (count - 1), [1] * (count - 1)
    while spare > 0:
        free = [i for i in range(count - 1) if counts[i] < reach]
        pool, left = sum([weights[i] for i in free]), spare
        for i in free:
            extra = min(reach - counts[i], max(1, left * weights[i] // pool), spare)
            counts[i] = counts[i] + extra
            spare = spare - extra
    return np.array([reach] + counts)


def uneven(key, count, total, most, lean):
    if count == 2:
        one = jax.random.randint(key, (), max(1, total - most), min(most, total - 1) + 1)
        return jnp.stack([one, total - one])
    sizes = jnp.asarray(split_up(count, total, most, lean), jnp.int32)
    pairs = (count - 1) // 2
    giver, sink = sizes[1:1 + 2 * pairs:2], sizes[2:2 + 2 * pairs:2]
    room = jnp.minimum(giver - 1, most - sink)
    moved = jax.random.randint(jax.random.fold_in(key, 1), (pairs,), 0, 1 << 20) % (room + 1)
    sizes = sizes.at[1:1 + 2 * pairs:2].set(giver - moved).at[2:2 + 2 * pairs:2].set(sink + moved)
    return sizes[jax.random.permutation(jax.random.fold_in(key, 2), count)]


def gaussian(rng, extent, spread, limit, cuts=(), held_as=jnp.bfloat16):
    drawn = spread * jax.random.normal(rng, extent, jnp.float32)
    if cuts:
        drawn = drawn * block_levels(rng, extent, cuts, -0.22, 0.18)
    return jnp.clip(drawn, -limit, limit).astype(held_as)


def setup_inputs(seed: int = 0) -> dict:
    seeds = jax.random.split(jax.random.key(seed), 10)
    return {
        "stream": gaussian(seeds[0], (MICRO, STREAM, CHANNELS), 1.0, 6.0, ((1, 32),)),
        "doc_ids": jax.vmap(lambda own: jnp.searchsorted(jnp.cumsum(uneven(own, DOCS, STREAM, STREAM // 2, 2)), jnp.arange(STREAM), side="right"))(jax.random.split(seeds[1], MICRO)).reshape((MICRO, STREAM)).astype(jnp.int32),
        "in_proj": gaussian(seeds[2], (LAYERS, CHANNELS, PROJ), CHANNELS ** -0.5, 0.09375, ((0, 8),)),
        "conv_weight": gaussian(seeds[3], (LAYERS, KERNEL, CHANNELS), KERNEL ** -0.5, 3.0, ((0, 8),), jnp.float32),
        "conv_bias": gaussian(seeds[4], (LAYERS, CHANNELS), 0.5, 3.0, ((0, 8),), jnp.float32),
        "decay_log": draw_decay_log(jax.random.fold_in(seeds[9], 71), 0),
        "step_bias": jnp.clip(-4.5 + 2.0 * jax.random.uniform(seeds[6], (LAYERS, HEADS), jnp.float32) ** block_levels(seeds[6], (LAYERS, HEADS), ((0, 8),), -0.2, 0.2), -4.5, -2.5),
        "skip_gain": jnp.clip(0.5 + 1.0 * jax.random.uniform(seeds[7], (LAYERS, HEADS), jnp.float32) ** block_levels(seeds[7], (LAYERS, HEADS), ((0, 8),), -0.2, 0.2), 0.5, 1.5),
        "norm_gain": jnp.clip(1.0 + 0.18 * jax.random.normal(seeds[8], (LAYERS, CHANNELS), jnp.float32), 0.1, 1.9),
    }


highest = lax.Precision.HIGHEST

def product(form, left, right):
    return jnp.einsum(form, left.astype(jnp.float32), right.astype(jnp.float32), precision=highest)

def conv_mix(padded, padded_ids, token_ids, conv_weight, conv_bias):
    length = token_ids.shape[0]
    summed = jnp.zeros((length, padded.shape[1]), jnp.float32)
    for offset in range(KERNEL):
        shifted = padded[offset:offset + length].astype(jnp.float32)
        same_doc = padded_ids[offset:offset + length] == token_ids
        summed = summed + conv_weight[offset][None, :] * jnp.where(same_doc[:, None], shifted, 0.0)
    return jax.nn.silu(summed + conv_bias[None, :]).astype(jnp.bfloat16)

def project(tokens, in_proj, step_bias):
    projected = jnp.dot(tokens, in_proj, preferred_element_type=jnp.float32)
    bc_width = GROUPS * STATE
    b_rows = projected[:, :bc_width].reshape(-1, GROUPS, STATE).astype(jnp.bfloat16)
    c_rows = projected[:, bc_width:2 * bc_width].reshape(-1, GROUPS, STATE).astype(jnp.bfloat16)
    step_size = jax.nn.softplus(projected[:, 2 * bc_width:] + step_bias[None, :])
    return (b_rows, c_rows, step_size)

def block_terms(inputs, b_rows, c_rows, step_size, log_decay, block_ids, prior_id):
    length = inputs.shape[0]
    per_group = HEADS // GROUPS
    running = jnp.cumsum(log_decay, axis=0)
    places = jnp.arange(length)
    inside = (block_ids[:, None] == block_ids[None, :]) & (places[:, None] >= places[None, :])
    decays = jnp.where(inside[:, :, None], jnp.exp(jnp.minimum(running[:, None, :] - running[None, :, :], 0.0)), 0.0)
    scores = product('tgn,sgn->tsg', c_rows, b_rows)
    weights = (scores[:, :, :, None] * (decays * step_size[None, :, :]).reshape(length, length, GROUPS, per_group)).astype(jnp.bfloat16)
    grouped = inputs.reshape(length, GROUPS, per_group, HEAD_DIM)
    intra_part = product('tsgj,sgjp->tgjp', weights, grouped).reshape(length, HEADS, HEAD_DIM)
    carry_gain = jnp.where((block_ids == prior_id)[:, None], jnp.exp(running), 0.0)
    tail_weight = jnp.where((block_ids == block_ids[-1])[:, None], jnp.exp(running[-1][None, :] - running), 0.0) * step_size
    scaled = (tail_weight.reshape(length, GROUPS, per_group)[:, :, :, None] * grouped.astype(jnp.float32)).astype(jnp.bfloat16)
    local_state = product('sgjp,sgn->gjpn', scaled, b_rows).reshape(HEADS, HEAD_DIM, STATE)
    return (intra_part, carry_gain, local_state, carry_gain[-1])

def carry_term(c_rows, carried, carry_gain):
    length = c_rows.shape[0]
    per_group = HEADS // GROUPS
    grouped = carried.astype(jnp.bfloat16).reshape(GROUPS, per_group, HEAD_DIM, STATE)
    carry_part = product('tgn,gjpn->tgjp', c_rows, grouped).reshape(length, HEADS, HEAD_DIM)
    return carry_part * carry_gain[:, :, None]

def finish(tokens, mixed_out, norm_gain):
    flat_mixed = mixed_out.reshape(tokens.shape[0], -1)
    inverse_rms = lax.rsqrt(lax.optimization_barrier(jnp.mean(flat_mixed * flat_mixed, axis=1, keepdims=True)) + 1e-05)
    return (tokens.astype(jnp.float32) + norm_gain[None, :] * flat_mixed * inverse_rms).astype(jnp.bfloat16)

def mamba_layer(tokens, token_ids, in_proj, conv_weight, conv_bias, decay_log, step_bias, skip_gain, norm_gain):
    length = tokens.shape[0]
    b_rows, c_rows, step_size = project(tokens, in_proj, step_bias)
    padded = jnp.concatenate([jnp.zeros((KERNEL - 1, tokens.shape[1]), tokens.dtype), tokens], axis=0)
    padded_ids = jnp.concatenate([jnp.full((KERNEL - 1,), -1, jnp.int32), token_ids.astype(jnp.int32)], axis=0)
    inputs = conv_mix(padded, padded_ids, token_ids, conv_weight, conv_bias).reshape(length, HEADS, HEAD_DIM)
    log_decay = -jnp.exp(decay_log)[None, :] * step_size
    blocks = length // TOK_DEV

    def shape_blocks(array_in):
        return array_in.reshape((blocks, TOK_DEV) + array_in.shape[1:])

    def advance(loop_carry, pieces):
        carried, prior_id = loop_carry
        block_in, block_b, block_c, block_step, block_decay, block_ids = pieces
        intra_part, carry_gain, local_state, end_gain = block_terms(block_in, block_b, block_c, block_step, block_decay, block_ids, prior_id)
        mixed_out = intra_part + carry_term(block_c, carried, carry_gain) + skip_gain[None, :, None] * block_in.astype(jnp.float32)
        return ((end_gain[:, None, None] * carried + local_state, block_ids[-1]), mixed_out)
    initial = (jnp.zeros((HEADS, HEAD_DIM, STATE), jnp.float32), jnp.int32(-1))
    pieces = tuple((shape_blocks(array_in) for array_in in (inputs, b_rows, c_rows, step_size, log_decay, token_ids.astype(jnp.int32))))
    final_carry, mixed_out = lax.scan(advance, initial, pieces)
    return finish(tokens, mixed_out.reshape(length, HEADS, HEAD_DIM), norm_gain)

def reference(stream, doc_ids, in_proj, conv_weight, conv_bias, decay_log, step_bias, skip_gain, norm_gain):
    columns = []
    for batch_index in range(MICRO):
        tokens = stream[batch_index]
        outputs = []
        for layer_index in range(LAYERS):
            tokens = mamba_layer(tokens, doc_ids[batch_index], in_proj[layer_index], conv_weight[layer_index], conv_bias[layer_index], decay_log[layer_index], step_bias[layer_index], skip_gain[layer_index], norm_gain[layer_index])
            outputs.append(tokens)
        columns.append(jnp.stack(outputs))
    return jnp.stack(columns, axis=1)
```

```python
import functools

import jax
import jax.numpy as jnp
from jax import lax
from jax.experimental import pallas as pl
from jax.experimental.pallas import tpu as pltpu
from jax.sharding import PartitionSpec as P

NY = 4
NC = 2
NX = 4
LAYERS = 8
HEADS = 64
HEAD_DIM = 64
STATE = 64
GROUPS = 4
KERNEL = 4
MICRO = 2
T = 128
CH = 1024
PER = 16
NCH = 8
REACH = 4
PROJ = 576
MESH = pl.DeviceIdType.MESH
F32 = jnp.float32
BF16 = jnp.bfloat16


def wait_bytes(ref, sem):
    pltpu.make_async_copy(ref, ref, sem).wait()


def kernel(
    nz,
    stream_ref,
    ids_ref,
    proj_ref,
    pp_ref,
    out_ref,
    wbuf,
    w0,
    strm,
    ubuf,
    gm,
    gmb,
    ppb,
    idsrc,
    idh,
    msk,
    halo,
    fbuf,
    inp,
    wts,
    bcu,
    bcm,
    bcuo,
    bcmo,
    su,
    sm,
    suo,
    smo,
    sg,
    lout,
    lrecv,
    gout,
    grecv,
    tout,
    ggout,
    trecv,
    ggrecv,
    rb,
    eout,
    ent,
    m0,
    gx,
    yr,
    ys,
    p0s,
    xr,
    xs,
    zr,
    zs,
    hr,
    hs,
    wr,
    wss,
    wrs,
    pps,
    outr,
    outs,
    idsem,
    loc,
):
    phase = lax.axis_index("phase")
    seg = lax.axis_index("seg")
    nseg = nz * NX
    y = phase // NC
    c = phase % NC
    z = seg // NX
    x = seg % NX

    def remote(src, dst, ssem, rsem, p, s):
        return pltpu.make_async_remote_copy(
            src_ref=src,
            dst_ref=dst,
            send_sem=ssem,
            recv_sem=rsem,
            device_id=(p, s),
            device_id_type=MESH,
        )

    barrier = pltpu.get_barrier_semaphore()
    count = 0
    for d in range(1, NY * NC):
        pl.semaphore_signal(barrier, inc=1, device_id=((phase + d) % (NY * NC), seg), device_id_type=MESH)
        count += 1
    for d in range(1, NX):
        pl.semaphore_signal(
            barrier, inc=1, device_id=(phase, z * NX + (x + d) % NX), device_id_type=MESH
        )
        count += 1
    for d in range(1, nz):
        pl.semaphore_signal(
            barrier, inc=1, device_id=(phase, ((z + d) % nz) * NX + x), device_id_type=MESH
        )
        count += 1
    for d in (1, nseg - 1):
        pl.semaphore_signal(barrier, inc=1, device_id=(phase, (seg + d) % nseg), device_id_type=MESH)
        count += 1

    cp_u = pltpu.make_async_copy(
        stream_ref.at[c, :, pl.ds(pl.multiple_of(y * CH, CH), CH)], ubuf.at[0], loc.at[0]
    )
    cp_u.start()
    cp_pp = pltpu.make_async_copy(pp_ref.at[y], ppb.at[phase], loc.at[1])
    cp_pp.start()

    @pl.when(phase == 0)
    def _():
        for k in range(4):
            pltpu.make_async_copy(proj_ref.at[0, pl.ds(k * CH, CH), :], w0.at[k], loc.at[3 + k]).start()
            pltpu.make_async_copy(
                stream_ref.at[:, :, pl.ds(k * CH, CH)], strm.at[k], loc.at[7 + k]
            ).start()

    @pl.when(phase > 0)
    def _():
        pltpu.make_async_copy(
            proj_ref.at[0, pl.ds(pl.multiple_of(y * CH, CH), CH), :], wbuf.at[phase - 1], loc.at[2]
        ).start()

    pl.semaphore_wait(barrier, count)

    idsrc[...] = jnp.broadcast_to(ids_ref[pl.ds(c, 1), :], (8, T))

    @pl.when(seg < nseg - 1)
    def _():
        remote(idsrc, idh, idsem.at[0], idsem.at[1], phase, seg + 1).start()

    @pl.when(seg == 0)
    def _():
        idh[...] = jnp.full((8, T), -1, jnp.int32)

    def send_params():
        for d in range(1, NY * NC):
            p = (phase + d) % (NY * NC)
            remote(pp_ref.at[p // NC], ppb.at[phase], pps.at[p], wr.at[phase, 2], p, seg).start()

    def send_weights():
        for dy in (2, 1, 3):
            yd = (y + dy) % NY
            remote(
                proj_ref.at[0, pl.ds(pl.multiple_of(yd * CH, CH), CH), :],
                wbuf.at[phase - 1],
                wss.at[yd],
                wr.at[phase, 0],
                yd * NC + c,
                seg,
            ).start()
        remote(
            proj_ref.at[0, pl.ds(pl.multiple_of(y * CH, CH), CH), :],
            wbuf.at[phase - 1],
            wss.at[y],
            wr.at[phase, 1],
            y * NC + 1 - c,
            seg,
        ).start()

    lane = lax.broadcasted_iota(jnp.int32, (T, 128), 1)
    low = lane < 64

    def split_rows(a):
        tiles = []
        for g in range(GROUPS):
            tb = a[:, 128 * (g // 2) : 128 * (g // 2) + 128]
            tc = a[:, 256 + 128 * (g // 2) : 256 + 128 * (g // 2) + 128]
            if g % 2 == 0:
                tiles.append(jnp.where(low, tb, pltpu.roll(tc, 64, 1)))
            else:
                tiles.append(jnp.where(low, pltpu.roll(tb, 64, 1), tc))
        return tiles

    @pl.when(phase == 0)
    def _():
        send_params()
        for k in range(4):
            pltpu.make_async_copy(proj_ref.at[0, pl.ds(k * CH, CH), :], w0.at[k], loc.at[3 + k]).wait()
            pltpu.make_async_copy(
                stream_ref.at[:, :, pl.ds(k * CH, CH)], strm.at[k], loc.at[7 + k]
            ).wait()
        for m in range(MICRO):
            at = LAYERS * m
            acc_bc = jnp.zeros((T, 512), F32)
            acc_s = jnp.zeros((T, 64), F32)
            for k in range(4):
                a = strm[k, m]
                acc_bc = acc_bc + jnp.dot(a, w0[k, :, 0:512], preferred_element_type=F32)
                acc_s = acc_s + jnp.dot(a, w0[k, :, 512:576], preferred_element_type=F32)
            tiles = split_rows(acc_bc)
            st = jnp.transpose(acc_s)
            for g in range(GROUPS):
                bcuo[at, g] = tiles[g].astype(BF16)
                suo[at, g] = st[16 * g : 16 * g + 16]
            for g in range(GROUPS):
                p = g * NC + m
                if p > 0:
                    remote(bcuo.at[at, g], bcu.at[0, 0], p0s.at[p, 0], yr.at[0, 0], p, seg).start()
                    remote(suo.at[at, g], su.at[0, 0], p0s.at[p, 1], yr.at[0, 1], p, seg).start()
        bcu[0, 0] = bcuo[0, 0]
        su[0, 0] = suo[0, 0]

    @pl.when(phase == 1)
    def _():
        send_params()
        send_weights()

    cp_u.wait()
    cp_pp.wait()

    @pl.when(phase > 0)
    def _():
        pltpu.make_async_copy(
            proj_ref.at[0, pl.ds(pl.multiple_of(y * CH, CH), CH), :], wbuf.at[phase - 1], loc.at[2]
        ).wait()

    bcm[0] = jnp.zeros((NY, T, 128), BF16)
    sm[0] = jnp.zeros((NY, 24, 128), F32)
    for s in range(1, NY):
        bcu[0, s] = jnp.zeros((T, 128), BF16)
        su[0, s] = jnp.zeros((16, 128), F32)
    gm[...] = jnp.zeros((T, CH), F32)

    @pl.when(seg > 0)
    def _():
        wait_bytes(idh, idsem.at[1])

    own_row = idsrc[...].astype(F32)
    prior_row = idh[...].astype(F32)
    lane8 = lax.broadcasted_iota(jnp.int32, (8, T), 1)
    row_rep = jnp.broadcast_to(own_row[0:1], (T, T))
    col_rep = jnp.transpose(row_rep)
    t_at = lax.broadcasted_iota(jnp.int32, (T, T), 0)
    msk[0] = jnp.where((row_rep == col_rep) & (t_at >= lane), 1.0, 0.0)
    for k in range(1, KERNEL):
        behind = jnp.where(lane8 < k, pltpu.roll(prior_row, k, 1), pltpu.roll(own_row, k, 1))
        same = jnp.where(behind == own_row, 1.0, 0.0)
        msk[k] = jnp.transpose(jnp.broadcast_to(same[0:1], (T, T)))
    prior_last = jnp.broadcast_to(prior_row[:, T - 1 : T], (8, T))
    own_last = jnp.broadcast_to(own_row[:, T - 1 : T], (8, T))
    sg[1, 0:8] = jnp.where(own_row == prior_last, 1.0, 0.0)
    sg[1, 8:16] = jnp.where(own_row == own_last, 1.0, 0.0)
    sum_up = jnp.where(t_at <= lane, 1.0, 0.0)

    def total_square(lx):
        s = sm[lx, 0, 16:24] + sm[lx, 1, 16:24] + sm[lx, 2, 16:24] + sm[lx, 3, 16:24]
        return lax.rsqrt(s * (1.0 / (CH * GROUPS)) + 1e-05)

    def new_tokens(lx, inv_rep):
        for j in range(NCH):
            cj = pl.ds(128 * j, 128)
            u = ubuf[lx, :, cj].astype(F32) + gm[:, cj] * inv_rep
            ub = u.astype(BF16)
            ubuf[lx + 1, :, cj] = ub
            fbuf[pl.ds(16, T), cj] = ub.astype(F32)

    def send_out(lx):
        there = out_ref.at[0, c, :, pl.ds(pl.multiple_of(y * CH, CH), CH)]

        @pl.when(phase == lx - 1)
        def _():
            pltpu.make_async_copy(ubuf.at[lx + 1], there, outs.at[lx]).start()

        @pl.when(phase != lx - 1)
        def _():
            remote(ubuf.at[lx + 1], there, outs.at[lx], outr.at[phase], lx - 1, seg).start()

    def wait_square(lx):
        wait_bytes(sm.at[lx, pl.ds(0, 3)], yr.at[lx, 3])

    def push_rows(lx, kind, outbuf, inbuf, soutbuf, sinbuf):
        for dy in (2, 1, 3):
            yd = (y + dy) % NY
            remote(
                outbuf.at[lx, yd], inbuf.at[lx, y], ys.at[lx, kind], yr.at[lx, kind], yd * NC + c, seg
            ).start()
        for dy in (2, 1, 3):
            yd = (y + dy) % NY
            remote(
                soutbuf.at[lx, yd],
                sinbuf.at[lx, y],
                ys.at[lx, kind + 1],
                yr.at[lx, kind + 1],
                yd * NC + c,
                seg,
            ).start()

    def conv_rows(l, r0, n):
        for j in range(NCH):
            cj = pl.ds(128 * j, 128)
            acc = fbuf[pl.ds(16 + r0, n), cj] * ppb[l, pl.ds(24 + j, 1), :] + ppb[l, pl.ds(32 + j, 1), :]
            for k in range(1, KERNEL):
                tap = ppb[l, pl.ds(8 * (3 - k) + j, 1), :]
                acc = acc + (fbuf[pl.ds(16 + r0 - k, n), cj] * msk[k, pl.ds(r0, n), :]) * tap
            inp[pl.ds(r0, n), cj] = (acc * (1.0 / (1.0 + jnp.exp(-acc)))).astype(BF16)

    def layer(l, carry):
        @pl.when(phase == l + 2)
        def _():
            send_params()
            send_weights()

        @pl.when((l == 0) & (phase > 0))
        def _():
            wait_bytes(bcu.at[0, 0], yr.at[0, 0])
            wait_bytes(su.at[0, 0], yr.at[0, 1])

        @pl.when(l > 0)
        def _():
            wait_bytes(bcu.at[l, pl.ds(0, 3)], yr.at[l, 0])
            wait_bytes(su.at[l, pl.ds(0, 3)], yr.at[l, 1])
            wait_bytes(bcm.at[l, pl.ds(0, 3)], yr.at[l, 2])
            wait_square(l)

        inv8 = total_square(l)
        inv_rep = jnp.transpose(jnp.broadcast_to(inv8[0:1], (T, T)))
        new_tokens(l, inv_rep)

        @pl.when(seg < nseg - 1)
        def _():
            remote(
                ubuf.at[l + 1, pl.ds(T - 16, 16), :], halo.at[l], hs.at[l], hr.at[l], phase, seg + 1
            ).start()

        @pl.when(l > 0)
        def _():
            send_out(l)

        @pl.when(phase != l)
        def _():
            wait_bytes(ppb.at[l], wr.at[l, 2])

        bc_u = (
            bcu[l, 0].astype(F32) + bcu[l, 1].astype(F32) + bcu[l, 2].astype(F32) + bcu[l, 3].astype(F32)
        )
        bc_m = (
            bcm[l, 0].astype(F32) + bcm[l, 1].astype(F32) + bcm[l, 2].astype(F32) + bcm[l, 3].astype(F32)
        )
        bc = (bc_u + inv_rep * bc_m).astype(BF16)
        bcf = bc.astype(F32)
        s_u = su[l, 0] + su[l, 1] + su[l, 2] + su[l, 3]
        s_m = sm[l, 0, 0:16] + sm[l, 1, 0:16] + sm[l, 2, 0:16] + sm[l, 3, 0:16]
        pre = s_u + inv8[0:1] * s_m + ppb[l, 72:88]
        step = jnp.maximum(pre, 0.0) + jnp.log1p(jnp.exp(-jnp.abs(pre)))
        log_decay = -jnp.exp(ppb[l, 56:72]) * step
        run = jnp.dot(log_decay, sum_up, preferred_element_type=F32, precision=lax.Precision.HIGHEST)
        goes_on = sg[1, 0:1]
        is_last = sg[1, 8:9]
        cgain = jnp.exp(run) * goes_on
        tail = jnp.exp(jnp.broadcast_to(run[:, T - 1 : T], (PER, T)) - run) * is_last * step
        sg[0] = jnp.broadcast_to(cgain[:, T - 1 : T], (PER, T))
        gain8 = jnp.where(
            lane8 < 64, sg[0, pl.ds(0, 8, stride=2), :], sg[0, pl.ds(1, 8, stride=2), :]
        )
        gout[l] = gain8
        grecv[l, x] = gain8
        for d in range(1, NX):
            xd = (x + d) % NX
            remote(gout.at[l], grecv.at[l, x], xs.at[l, 1], xr.at[l, 1], phase, z * NX + xd).start()

        bct = jnp.transpose(bcf)
        bt = bct[0:64]
        cfull = jnp.where(low, pltpu.roll(bcf, 64, 1), 0.0).astype(BF16)
        scores = lax.dot_general(cfull, bc, (((1,), (1,)), ((), ())), preferred_element_type=F32)
        scores = scores * msk[0]
        cols = jnp.transpose(jnp.concatenate([run, cgain, jnp.zeros((T - 2 * PER, T), F32)], axis=0))
        for j in range(NCH):
            for i in range(2):
                h = 2 * j + i
                gap = jnp.broadcast_to(cols[:, h : h + 1], (T, T)) - run[h : h + 1]
                w = scores * (jnp.exp(jnp.minimum(gap, 0.0)) * step[h : h + 1])
                wts[j, :, pl.ds(128 * i, 128)] = w.astype(BF16)
            g0 = jnp.broadcast_to(cols[:, PER + 2 * j : PER + 2 * j + 1], (T, T))
            g1 = jnp.broadcast_to(cols[:, PER + 2 * j + 1 : PER + 2 * j + 2], (T, T))
            gx[:, pl.ds(128 * j, 128)] = jnp.where(low, g0, g1)

        conv_rows(l, 16, T - 16)

        @pl.when(seg > 0)
        def _():
            wait_bytes(halo.at[l], hr.at[l])

        @pl.when(seg == 0)
        def _():
            halo[l] = jnp.zeros((16, CH), BF16)

        fbuf[pl.ds(0, 16), :] = halo[l].astype(F32)
        conv_rows(l, 0, 16)

        low64 = low[0:64]
        for j in range(NCH):
            cj = pl.ds(128 * j, 128)
            left = jnp.concatenate([bt * tail[2 * j : 2 * j + 1], bt * tail[2 * j + 1 : 2 * j + 2]], axis=0)
            both = jnp.dot(left.astype(BF16), inp[:, cj], preferred_element_type=F32)
            st = jnp.where(low64, both[0:64], both[64:128]).astype(BF16)
            for q in range(NX):
                lout[l, q, :, cj] = st[16 * q : 16 * q + 16]
        for d in (2, 1, 3):
            xd = (x + d) % NX
            remote(
                lout.at[l, xd], lrecv.at[l, x], xs.at[l, 0], xr.at[l, 0], phase, z * NX + xd
            ).start()
        lrecv[l, x] = lout[l, x]

        for j in range(NCH):
            cj = pl.ds(128 * j, 128)
            v = inp[:, cj]
            vf = v.astype(F32)
            right = jnp.concatenate([jnp.where(low, vf, 0.0), jnp.where(low, 0.0, vf)], axis=0).astype(BF16)
            intra = jnp.dot(wts[j], right, preferred_element_type=F32)
            m0[:, cj] = intra + ppb[l, pl.ds(48 + j, 1), :] * vf

        wait_bytes(grecv.at[l, pl.ds(0, 3)], xr.at[l, 1])
        wait_bytes(lrecv.at[l, pl.ds(0, 3)], xr.at[l, 0])
        p1 = grecv[l, 0]
        p2 = p1 * grecv[l, 1]
        p3 = p2 * grecv[l, 2]
        ggout[l] = p3 * grecv[l, 3]
        ga = grecv[l, 1]
        gb = grecv[l, 2]
        gc = grecv[l, 3]
        for j in range(NCH):
            cj = pl.ds(128 * j, 128)
            r1 = lrecv[l, 0, :, cj].astype(F32)
            r2 = lrecv[l, 1, :, cj].astype(F32) + ga[j : j + 1] * r1
            r3 = lrecv[l, 2, :, cj].astype(F32) + gb[j : j + 1] * r2
            rt = lrecv[l, 3, :, cj].astype(F32) + gc[j : j + 1] * r3
            rb[0, :, cj] = r1
            rb[1, :, cj] = r2
            rb[2, :, cj] = r3
            tout[l, :, cj] = rt.astype(BF16)
        for d in range(REACH, 0, -1):

            @pl.when(z + d < nz)
            def _(d=d):
                to = (z + d) * NX + x
                remote(
                    ggout.at[l], ggrecv.at[l, d - 1], zs.at[l, REACH + d - 1], zr.at[l, REACH + d - 1], phase, to
                ).start()
                remote(tout.at[l], trecv.at[l, d - 1], zs.at[l, d - 1], zr.at[l, d - 1], phase, to).start()

        n = l + 1
        yo = n // NC
        co = n % NC

        @pl.when(n < LAYERS)
        def _():
            @pl.when((c == co) & (y != yo))
            def _():
                wait_bytes(wbuf.at[l], wr.at[n, 0])
                remote(wbuf.at[l], wbuf.at[l], wrs.at[l], wr.at[n, 1], y * NC + 1 - c, seg).start()

            @pl.when(c != co)
            def _():
                wait_bytes(wbuf.at[l], wr.at[n, 1])

            a = ubuf[l + 1]
            tiles = split_rows(jnp.dot(a, wbuf[l, :, 0:512], preferred_element_type=F32))
            st = jnp.transpose(jnp.dot(a, wbuf[l, :, 512:576], preferred_element_type=F32))
            for g in range(GROUPS):
                bcuo[n, g] = tiles[g].astype(BF16)
                suo[n, g] = st[16 * g : 16 * g + 16]
            bcu[n, y] = bcuo[n, y]
            su[n, y] = suo[n, y]
            push_rows(n, 0, bcuo, bcu, suo, su)

        for d in range(1, REACH + 1):

            @pl.when(z >= d)
            def _(d=d):
                wait_bytes(ggrecv.at[l, d - 1], zr.at[l, REACH + d - 1])
                wait_bytes(trecv.at[l, d - 1], zr.at[l, d - 1])

            @pl.when(z < d)
            def _(d=d):
                ggrecv[l, d - 1] = jnp.zeros((8, 128), F32)
                trecv[l, d - 1] = jnp.zeros((16, CH), BF16)

        for j in range(NCH):
            cj = pl.ds(128 * j, 128)
            e = trecv[l, 3, :, cj].astype(F32)
            for d in (2, 1, 0):
                e = trecv[l, d, :, cj].astype(F32) + ggrecv[l, d, pl.ds(j, 1), :] * e
            eout[l, 0, :, cj] = e.astype(BF16)
            eout[l, 1, :, cj] = (rb[0, :, cj] + p1[j : j + 1] * e).astype(BF16)
            eout[l, 2, :, cj] = (rb[1, :, cj] + p2[j : j + 1] * e).astype(BF16)
            eout[l, 3, :, cj] = (rb[2, :, cj] + p3[j : j + 1] * e).astype(BF16)
        for d in (2, 1, 3):
            xd = (x + d) % NX
            remote(
                eout.at[l, xd], ent.at[l, x], xs.at[l, 2], xr.at[l, 2], phase, z * NX + xd
            ).start()
        ent[l, x] = eout[l, x]

        wait_bytes(ent.at[l, pl.ds(0, 3)], xr.at[l, 2])
        cs = cfull[:, 0:64]
        sq = jnp.zeros((T, 128), F32)
        for j in range(NCH):
            cj = pl.ds(128 * j, 128)
            part = jnp.dot(cs, ent[l, :, :, cj].reshape(STATE, 128), preferred_element_type=F32)
            mixed = m0[:, cj] + part * gx[:, cj]
            sq = sq + mixed * mixed
            scaled = ppb[l, pl.ds(40 + j, 1), :] * mixed
            gm[:, cj] = scaled
            gmb[:, cj] = scaled.astype(BF16)
        sq_row = jnp.broadcast_to(jnp.sum(jnp.transpose(sq), axis=0, keepdims=True), (8, T))
        for g in range(GROUPS):
            smo[n, g, 16:24] = sq_row

        @pl.when(n < LAYERS)
        def _():
            a = gmb[...]
            tiles = split_rows(jnp.dot(a, wbuf[l, :, 0:512], preferred_element_type=F32))
            st = jnp.transpose(jnp.dot(a, wbuf[l, :, 512:576], preferred_element_type=F32))
            for g in range(GROUPS):
                bcmo[n, g] = tiles[g].astype(BF16)
                smo[n, g, 0:16] = st[16 * g : 16 * g + 16]
            bcm[n, y] = bcmo[n, y]
            sm[n, y] = smo[n, y]
            push_rows(n, 2, bcmo, bcm, smo, sm)

        @pl.when(n == LAYERS)
        def _():
            for g in range(GROUPS):
                smo[n, g, 0:16] = jnp.zeros((16, 128), F32)
            sm[n, y] = smo[n, y]
            for dy in (2, 1, 3):
                yd = (y + dy) % NY
                remote(
                    smo.at[n, yd], sm.at[n, y], ys.at[n, 3], yr.at[n, 3], yd * NC + c, seg
                ).start()

        return carry

    lax.fori_loop(0, LAYERS, layer, 0)

    wait_square(LAYERS)
    inv8 = total_square(LAYERS)
    new_tokens(LAYERS, jnp.transpose(jnp.broadcast_to(inv8[0:1], (T, T))))
    send_out(LAYERS)

    def drain(l, carry):
        n = l + 1

        @pl.when(n < LAYERS)
        def _():
            wait_bytes(bcuo.at[n, pl.ds(0, 3)], ys.at[n, 0])
            wait_bytes(suo.at[n, pl.ds(0, 3)], ys.at[n, 1])
            wait_bytes(bcmo.at[n, pl.ds(0, 3)], ys.at[n, 2])

        wait_bytes(smo.at[n, pl.ds(0, 3)], ys.at[n, 3])
        wait_bytes(ubuf.at[n + 1], outs.at[n])
        wait_bytes(lout.at[l, pl.ds(0, 3)], xs.at[l, 0])
        wait_bytes(grecv.at[l, pl.ds(0, 3)], xs.at[l, 1])
        wait_bytes(eout.at[l, pl.ds(0, 3)], xs.at[l, 2])
        for d in range(1, REACH + 1):

            @pl.when(z + d < nz)
            def _(d=d):
                wait_bytes(ggout.at[l], zs.at[l, REACH + d - 1])
                wait_bytes(tout.at[l], zs.at[l, d - 1])

        @pl.when(seg < nseg - 1)
        def _():
            wait_bytes(halo.at[l], hs.at[l])

        @pl.when((n < LAYERS) & (c == n % NC) & (y != n // NC))
        def _():
            wait_bytes(wbuf.at[l], wrs.at[l])

        @pl.when(phase != l)
        def _():
            wait_bytes(ubuf.at[0], outr.at[l])
            wait_bytes(ppb.at[l], pps.at[l])

        return carry

    lax.fori_loop(0, LAYERS, drain, 0)

    @pl.when(phase > 0)
    def _():
        for yd in range(NY):
            wait_bytes(wbuf.at[0], wss.at[yd])

    @pl.when(phase == 0)
    def _():
        for p in range(1, NY * NC):
            wait_bytes(bcuo.at[0, 0], p0s.at[p, 0])
            wait_bytes(suo.at[0, 0], p0s.at[p, 1])

    @pl.when(seg < nseg - 1)
    def _():
        wait_bytes(idsrc, idsem.at[0])


def body(
    stream, doc_ids, in_proj, conv_weight, conv_bias, decay_log, step_bias, skip_gain, norm_gain
):
    nseg = lax.axis_size("seg")
    nz = nseg // NX

    def rows(a):
        return a.reshape(-1, GROUPS, NCH, 128).transpose(1, 0, 2, 3).reshape(GROUPS, -1, 128)

    def wide(a):
        return jnp.broadcast_to(a.reshape(GROUPS, PER, 1), (GROUPS, PER, 128))

    params = jnp.concatenate(
        [
            rows(conv_weight[0]),
            rows(conv_bias),
            rows(norm_gain),
            rows(jnp.repeat(skip_gain, HEAD_DIM, axis=1)),
            wide(decay_log),
            wide(step_bias),
        ],
        axis=1,
    )
    vmem = pltpu.VMEM
    dma = pltpu.SemaphoreType.DMA
    n1 = LAYERS + 1
    return pl.pallas_call(
        functools.partial(kernel, nz),
        out_shape=jax.ShapeDtypeStruct((1, MICRO, T, CH * GROUPS), BF16),
        in_specs=[
            pl.BlockSpec(memory_space=pl.ANY),
            pl.BlockSpec(memory_space=pltpu.VMEM),
            pl.BlockSpec(memory_space=pl.ANY),
            pl.BlockSpec(memory_space=pl.ANY),
        ],
        out_specs=pl.BlockSpec(memory_space=pl.ANY),
        scratch_shapes=[
            vmem((LAYERS - 1, CH, PROJ), BF16),
            vmem((4, CH, PROJ), BF16),
            vmem((4, MICRO, T, CH), BF16),
            vmem((LAYERS + 2, T, CH), BF16),
            vmem((T, CH), F32),
            vmem((T, CH), BF16),
            vmem((LAYERS, 88, 128), F32),
            vmem((8, T), jnp.int32),
            vmem((8, T), jnp.int32),
            vmem((KERNEL, T, T), F32),
            vmem((LAYERS, 16, CH), BF16),
            vmem((T + 16, CH), F32),
            vmem((T, CH), BF16),
            vmem((NCH, T, 256), BF16),
            vmem((n1, NY, T, 128), BF16),
            vmem((n1, NY, T, 128), BF16),
            vmem((n1, NY, T, 128), BF16),
            vmem((n1, NY, T, 128), BF16),
            vmem((n1, NY, 16, 128), F32),
            vmem((n1, NY, 24, 128), F32),
            vmem((n1, NY, 16, 128), F32),
            vmem((n1, NY, 24, 128), F32),
            vmem((2, 16, 128), F32),
            vmem((LAYERS, NX, 16, CH), BF16),
            vmem((LAYERS, NX, 16, CH), BF16),
            vmem((LAYERS, 8, 128), F32),
            vmem((LAYERS, NX, 8, 128), F32),
            vmem((LAYERS, 16, CH), BF16),
            vmem((LAYERS, 8, 128), F32),
            vmem((LAYERS, REACH, 16, CH), BF16),
            vmem((LAYERS, REACH, 8, 128), F32),
            vmem((3, 16, CH), F32),
            vmem((LAYERS, NX, 16, CH), BF16),
            vmem((LAYERS, NX, 16, CH), BF16),
            vmem((T, CH), F32),
            vmem((T, CH), F32),
            dma((n1, 4)),
            dma((n1, 4)),
            dma((NY * NC, 2)),
            dma((LAYERS, 3)),
            dma((LAYERS, 3)),
            dma((LAYERS, 2 * REACH)),
            dma((LAYERS, 2 * REACH)),
            dma((LAYERS,)),
            dma((LAYERS,)),
            dma((LAYERS, 3)),
            dma((NY,)),
            dma((LAYERS,)),
            dma((NY * NC,)),
            dma((NY * NC,)),
            dma((n1,)),
            dma((2,)),
            dma((11,)),
        ],
        compiler_params=pltpu.CompilerParams(
            collective_id=0, has_side_effects=True, vmem_limit_bytes=60 * 1024 * 1024
        ),
    )(stream, doc_ids, in_proj, params)


def solution(mesh):
    placed = (
        P(None, "seg", None),
        P(None, "seg"),
        P("phase", None, None),
        P("phase", None, None),
        P("phase", None),
        P("phase", None),
        P("phase", None),
        P("phase", None),
        P("phase", None),
    )
    return jax.shard_map(
        body, mesh=mesh, in_specs=placed, out_specs=P("phase", None, "seg", None), check_vma=False
    )
```

```python
import functools

import jax
import jax.numpy as jnp
from jax import lax
from jax.experimental import pallas as pl
from jax.experimental.pallas import tpu as pltpu
from jax.sharding import PartitionSpec as P

NY = 4
NC = 2
NX = 4
LAYERS = 8
HEADS = 64
HEAD_DIM = 64
STATE = 64
GROUPS = 4
KERNEL = 4
MICRO = 2
T = 128
CH = 1024
PER = 16
NCH = 8
REACH = 4
PROJ = 576
WPART = 144
WHALF = 80
MESH = pl.DeviceIdType.MESH
F32 = jnp.float32
BF16 = jnp.bfloat16


def wait_bytes(ref, sem):
    pltpu.make_async_copy(ref, ref, sem).wait()


def kernel(
    nz,
    stream_ref,
    ids_ref,
    proj_ref,
    convw_ref,
    convb_ref,
    decay_ref,
    stepb_ref,
    skip_ref,
    norm_ref,
    out_ref,
    wbuf,
    w0,
    strm,
    ubuf,
    gm,
    gmb,
    pps,
    pph,
    p0,
    ppb,
    idsrc,
    idh,
    msk,
    halo,
    fbuf,
    inp,
    wts,
    bcu,
    bcm,
    bcuo,
    bcmo,
    su,
    sm,
    suo,
    smo,
    sg,
    lout,
    lrecv,
    gout,
    grecv,
    tout,
    ggout,
    trecv,
    ggrecv,
    rb,
    eout,
    ent,
    m0,
    gx,
    yr,
    ys,
    p0s,
    xr,
    xs,
    zr,
    zs,
    hr,
    hs,
    wr,
    wss,
    wrs,
    wxs,
    ppsem,
    outr,
    outs,
    idsem,
    loc,
):
    phase = lax.axis_index("phase")
    seg = lax.axis_index("seg")
    nseg = nz * NX
    y = phase // NC
    c = phase % NC
    z = seg // NX
    x = seg % NX

    def remote(src, dst, ssem, rsem, p, s):
        return pltpu.make_async_remote_copy(
            src_ref=src,
            dst_ref=dst,
            send_sem=ssem,
            recv_sem=rsem,
            device_id=(p, s),
            device_id_type=MESH,
        )

    barrier = pltpu.get_barrier_semaphore()
    count = 0
    for d in range(1, NY * NC):
        pl.semaphore_signal(barrier, inc=1, device_id=((phase + d) % (NY * NC), seg), device_id_type=MESH)
        count += 1
    for d in range(1, NX):
        pl.semaphore_signal(
            barrier, inc=1, device_id=(phase, z * NX + (x + d) % NX), device_id_type=MESH
        )
        count += 1
    for d in range(1, nz):
        pl.semaphore_signal(
            barrier, inc=1, device_id=(phase, ((z + d) % nz) * NX + x), device_id_type=MESH
        )
        count += 1
    for d in (1, nseg - 1):
        pl.semaphore_signal(barrier, inc=1, device_id=(phase, (seg + d) % nseg), device_id_type=MESH)
        count += 1

    cp_u = pltpu.make_async_copy(
        stream_ref.at[c, :, pl.ds(pl.multiple_of(y * CH, CH), CH)], ubuf.at[0], loc.at[0]
    )
    cp_u.start()
    def quarter(g):
        return proj_ref.at[0, :, pl.ds(pl.multiple_of(g * CH, CH), CH)]

    cp_w0 = pltpu.make_async_copy(proj_ref.at[0], w0, loc.at[1])
    cp_s0 = pltpu.make_async_copy(stream_ref, strm, loc.at[3])

    @pl.when(phase == 0)
    def _():
        cp_w0.start()
        cp_s0.start()

    @pl.when(phase > 0)
    def _():
        pltpu.make_async_copy(quarter(y), wbuf.at[phase - 1], loc.at[2]).start()

    low8 = lax.broadcasted_iota(jnp.int32, (8, 128), 1) < 64
    for g in range(GROUPS):
        for j in range(NCH):
            cj = pl.ds(CH * g + 128 * j, 128)
            for k in range(KERNEL):
                pps[g, pl.ds(8 * k + j, 1), :] = convw_ref[0, pl.ds(k, 1), cj]
            pps[g, pl.ds(32 + j, 1), :] = convb_ref[:, cj]
            pps[g, pl.ds(40 + j, 1), :] = norm_ref[:, cj]

    def per_head(ref):
        return jnp.transpose(jnp.broadcast_to(ref[...], (128, HEADS)))

    pph[...] = per_head(skip_ref)
    decay_rows = per_head(decay_ref)
    stepb_rows = per_head(stepb_ref)
    for g in range(GROUPS):
        pps[g, 48:56] = jnp.where(
            low8, pph[pl.ds(PER * g, 8, stride=2), :], pph[pl.ds(PER * g + 1, 8, stride=2), :]
        )
        pps[g, 56:72] = decay_rows[PER * g : PER * g + PER]
        pps[g, 72:88] = stepb_rows[PER * g : PER * g + PER]
    ppb[phase] = pps[y]

    pl.semaphore_wait(barrier, count)

    idsrc[...] = jnp.broadcast_to(ids_ref[pl.ds(c, 1), :], (8, T))

    @pl.when(seg < nseg - 1)
    def _():
        remote(idsrc, idh, idsem.at[0], idsem.at[1], phase, seg + 1).start()

    @pl.when(seg == 0)
    def _():
        idh[...] = jnp.full((8, T), -1, jnp.int32)

    def send_params():
        for d in range(1, NY * NC):
            p = (phase + d) % (NY * NC)
            remote(pps.at[p // NC], ppb.at[phase], ppsem.at[p], wr.at[phase, 6], p, seg).start()

    def part(n, i, r0, rows):
        return wbuf.at[n - 1, pl.ds(pl.multiple_of(i * WPART + r0, 16), rows), :]

    def send_weights():
        rows = pl.ds(pl.multiple_of(x * WPART, 16), WPART)
        for dy in (2, 1, 3):
            yd = (y + dy) % NY
            remote(
                proj_ref.at[0, rows, pl.ds(pl.multiple_of(yd * CH, CH), CH)],
                part(phase, x, 0, WPART),
                wss.at[yd],
                wr.at[phase, 0],
                yd * NC + c,
                seg,
            ).start()
        remote(quarter(y), wbuf.at[phase - 1], wss.at[y], wr.at[phase, 5], y * NC + 1 - c, seg).start()

    def relays(n):
        return (n < LAYERS) & (c == n % NC) & (y != n // NC)

    right = z * NX + (x + 1) % NX
    left = z * NX + (x + NX - 1) % NX

    def weights_1(n):
        @pl.when(relays(n))
        def _():
            mine = part(n, x, 0, WPART)
            wait_bytes(mine, wr.at[n, 0])
            remote(mine, mine, wxs.at[n, 0], wr.at[n, 1], phase, right).start()
            remote(mine, mine, wxs.at[n, 1], wr.at[n, 2], phase, left).start()

    def weights_2(n):
        @pl.when(relays(n))
        def _():
            wait_bytes(part(n, x, 0, WPART), wr.at[n, 1])
            first = part(n, (x + NX - 1) % NX, 0, WHALF)
            remote(first, first, wxs.at[n, 2], wr.at[n, 3], phase, right).start()
            wait_bytes(part(n, x, 0, WPART), wr.at[n, 2])
            last = part(n, (x + 1) % NX, WHALF, WPART - WHALF)
            remote(last, last, wxs.at[n, 3], wr.at[n, 4], phase, left).start()

    def weights_3(n):
        @pl.when(relays(n))
        def _():
            wait_bytes(part(n, x, 0, WHALF), wr.at[n, 3])
            wait_bytes(part(n, x, 0, WPART - WHALF), wr.at[n, 4])
            whole = wbuf.at[n - 1]
            remote(whole, whole, wrs.at[n], wr.at[n, 5], y * NC + 1 - c, seg).start()

        @pl.when((n < LAYERS) & (c != n % NC))
        def _():
            wait_bytes(wbuf.at[n - 1], wr.at[n, 5])

    lane = lax.broadcasted_iota(jnp.int32, (T, 128), 1)
    low = lane < 64

    def product(w, a):
        return lax.dot_general(w, a, (((1,), (1,)), ((), ())), preferred_element_type=F32)

    def rows_of(a, g):
        return jnp.concatenate(
            [a[64 * g : 64 * g + 64], a[256 + 64 * g : 320 + 64 * g]], axis=0
        ).astype(BF16)

    @pl.when(phase == 0)
    def _():
        send_params()
        cp_w0.wait()
        cp_s0.wait()
        both = strm[...].reshape(MICRO * T, CH * GROUPS)
        for r in range(4):
            rr = pl.ds(WPART * r, WPART)
            p0[rr, :] = product(w0[rr, :], both)
        for m in range(MICRO):
            at = LAYERS * m
            cm = pl.ds(T * m, T)
            for g in range(GROUPS):
                bcuo[at, g, 0:64] = p0[pl.ds(64 * g, 64), cm].astype(BF16)
                bcuo[at, g, 64:128] = p0[pl.ds(256 + 64 * g, 64), cm].astype(BF16)
                suo[at, g] = p0[pl.ds(512 + 16 * g, 16), cm]
            for g in (2, 1, 3, 0):
                p = g * NC + m
                if p > 0:
                    remote(bcuo.at[at, g], bcu.at[0, 0], p0s.at[p, 0], yr.at[0, 0], p, seg).start()
                    remote(suo.at[at, g], su.at[0, 0], p0s.at[p, 1], yr.at[0, 1], p, seg).start()
        bcu[0, 0] = bcuo[0, 0]
        su[0, 0] = suo[0, 0]

    @pl.when((phase == 1) | (phase == 2))
    def _():
        send_params()
        send_weights()

    cp_u.wait()

    @pl.when(phase > 0)
    def _():
        pltpu.make_async_copy(quarter(y), wbuf.at[phase - 1], loc.at[2]).wait()

    bcm[0] = jnp.zeros((NY, T, 128), BF16)
    sm[0] = jnp.zeros((NY, 24, 128), F32)
    for s in range(1, NY):
        bcu[0, s] = jnp.zeros((T, 128), BF16)
        su[0, s] = jnp.zeros((16, 128), F32)
    gm[...] = jnp.zeros((T, CH), F32)

    @pl.when(seg > 0)
    def _():
        wait_bytes(idh, idsem.at[1])

    own_row = idsrc[...].astype(F32)
    prior_row = idh[...].astype(F32)
    lane8 = lax.broadcasted_iota(jnp.int32, (8, T), 1)
    row_rep = jnp.broadcast_to(own_row[0:1], (T, T))
    col_rep = jnp.transpose(row_rep)
    t_at = lax.broadcasted_iota(jnp.int32, (T, T), 0)
    msk[0] = jnp.where((row_rep == col_rep) & (t_at >= lane), 1.0, 0.0)
    for k in range(1, KERNEL):
        behind = jnp.where(lane8 < k, pltpu.roll(prior_row, k, 1), pltpu.roll(own_row, k, 1))
        same = jnp.where(behind == own_row, 1.0, 0.0)
        msk[k] = jnp.transpose(jnp.broadcast_to(same[0:1], (T, T)))
    prior_last = jnp.broadcast_to(prior_row[:, T - 1 : T], (8, T))
    own_last = jnp.broadcast_to(own_row[:, T - 1 : T], (8, T))
    sg[1, 0:8] = jnp.where(own_row == prior_last, 1.0, 0.0)
    sg[1, 8:16] = jnp.where(own_row == own_last, 1.0, 0.0)
    sum_up = jnp.where(t_at <= lane, 1.0, 0.0)
    weights_1(1)

    def total_square(lx):
        s = sm[lx, 0, 16:24] + sm[lx, 1, 16:24] + sm[lx, 2, 16:24] + sm[lx, 3, 16:24]
        return lax.rsqrt(s * (1.0 / (CH * GROUPS)) + 1e-05)

    def new_tokens(lx, inv_rep):
        for j in range(NCH):
            cj = pl.ds(128 * j, 128)
            u = ubuf[lx, :, cj].astype(F32) + gm[:, cj] * inv_rep
            ub = u.astype(BF16)
            ubuf[lx + 1, :, cj] = ub
            fbuf[pl.ds(16, T), cj] = ub.astype(F32)

    def send_out(lx):
        there = out_ref.at[0, c, :, pl.ds(pl.multiple_of(y * CH, CH), CH)]

        @pl.when(phase == lx - 1)
        def _():
            pltpu.make_async_copy(ubuf.at[lx + 1], there, outs.at[lx]).start()

        @pl.when(phase != lx - 1)
        def _():
            remote(ubuf.at[lx + 1], there, outs.at[lx], outr.at[phase], lx - 1, seg).start()

    def wait_square(lx):
        wait_bytes(sm.at[lx, pl.ds(0, 3)], yr.at[lx, 3])

    def push_rows(lx, kind, outbuf, inbuf, soutbuf, sinbuf):
        for dy in (2, 1, 3):
            yd = (y + dy) % NY
            remote(
                outbuf.at[lx, yd], inbuf.at[lx, y], ys.at[lx, kind], yr.at[lx, kind], yd * NC + c, seg
            ).start()
        for dy in (2, 1, 3):
            yd = (y + dy) % NY
            remote(
                soutbuf.at[lx, yd],
                sinbuf.at[lx, y],
                ys.at[lx, kind + 1],
                yr.at[lx, kind + 1],
                yd * NC + c,
                seg,
            ).start()

    def conv_rows(l, r0, n):
        for j in range(NCH):
            cj = pl.ds(128 * j, 128)
            acc = fbuf[pl.ds(16 + r0, n), cj] * ppb[l, pl.ds(24 + j, 1), :] + ppb[l, pl.ds(32 + j, 1), :]
            for k in range(1, KERNEL):
                tap = ppb[l, pl.ds(8 * (3 - k) + j, 1), :]
                acc = acc + (fbuf[pl.ds(16 + r0 - k, n), cj] * msk[k, pl.ds(r0, n), :]) * tap
            inp[pl.ds(r0, n), cj] = (acc * (1.0 / (1.0 + jnp.exp(-acc)))).astype(BF16)

    def layer(l, carry):
        @pl.when(phase == l + 3)
        def _():
            send_params()
            send_weights()

        @pl.when((l == 0) & (phase > 0))
        def _():
            wait_bytes(bcu.at[0, 0], yr.at[0, 0])
            wait_bytes(su.at[0, 0], yr.at[0, 1])

        @pl.when(l > 0)
        def _():
            wait_bytes(bcu.at[l, pl.ds(0, 3)], yr.at[l, 0])
            wait_bytes(su.at[l, pl.ds(0, 3)], yr.at[l, 1])
            wait_bytes(bcm.at[l, pl.ds(0, 3)], yr.at[l, 2])
            wait_square(l)

        inv8 = total_square(l)
        inv_rep = jnp.transpose(jnp.broadcast_to(inv8[0:1], (T, T)))
        new_tokens(l, inv_rep)

        @pl.when(seg < nseg - 1)
        def _():
            remote(
                ubuf.at[l + 1, pl.ds(T - 16, 16), :], halo.at[l], hs.at[l], hr.at[l], phase, seg + 1
            ).start()

        @pl.when(l > 0)
        def _():
            send_out(l)

        @pl.when(phase != l)
        def _():
            wait_bytes(ppb.at[l], wr.at[l, 6])

        bc_u = (
            bcu[l, 0].astype(F32) + bcu[l, 1].astype(F32) + bcu[l, 2].astype(F32) + bcu[l, 3].astype(F32)
        )
        bc_m = (
            bcm[l, 0].astype(F32) + bcm[l, 1].astype(F32) + bcm[l, 2].astype(F32) + bcm[l, 3].astype(F32)
        )
        bc = (bc_u + inv8[0:1] * bc_m).astype(BF16)
        bt = bc[0:64].astype(F32)
        cs = jnp.transpose(bc[64:128].astype(F32)).astype(BF16)
        s_u = su[l, 0] + su[l, 1] + su[l, 2] + su[l, 3]
        s_m = sm[l, 0, 0:16] + sm[l, 1, 0:16] + sm[l, 2, 0:16] + sm[l, 3, 0:16]
        pre = s_u + inv8[0:1] * s_m + ppb[l, 72:88]
        step = jnp.maximum(pre, 0.0) + jnp.log1p(jnp.exp(-jnp.abs(pre)))
        log_decay = -jnp.exp(ppb[l, 56:72]) * step
        run = jnp.dot(log_decay, sum_up, preferred_element_type=F32, precision=lax.Precision.HIGHEST)
        goes_on = sg[1, 0:1]
        is_last = sg[1, 8:9]
        cgain = jnp.exp(run) * goes_on
        tail = jnp.exp(jnp.broadcast_to(run[:, T - 1 : T], (PER, T)) - run) * is_last * step
        sg[0] = jnp.broadcast_to(cgain[:, T - 1 : T], (PER, T))
        gain8 = jnp.where(
            lane8 < 64, sg[0, pl.ds(0, 8, stride=2), :], sg[0, pl.ds(1, 8, stride=2), :]
        )
        gout[l] = gain8
        grecv[l, x] = gain8
        for d in range(1, NX):
            xd = (x + d) % NX
            remote(gout.at[l], grecv.at[l, x], xs.at[l, 1], xr.at[l, 1], phase, z * NX + xd).start()

        scores = jnp.dot(cs, bc[0:64], preferred_element_type=F32)
        scores = scores * msk[0]
        cols = jnp.transpose(jnp.concatenate([run, cgain, jnp.zeros((T - 2 * PER, T), F32)], axis=0))
        for j in range(NCH):
            for i in range(2):
                h = 2 * j + i
                gap = jnp.broadcast_to(cols[:, h : h + 1], (T, T)) - run[h : h + 1]
                w = scores * (jnp.exp(jnp.minimum(gap, 0.0)) * step[h : h + 1])
                wts[j, :, pl.ds(128 * i, 128)] = w.astype(BF16)
            g0 = jnp.broadcast_to(cols[:, PER + 2 * j : PER + 2 * j + 1], (T, T))
            g1 = jnp.broadcast_to(cols[:, PER + 2 * j + 1 : PER + 2 * j + 2], (T, T))
            gx[:, pl.ds(128 * j, 128)] = jnp.where(low, g0, g1)

        conv_rows(l, 16, T - 16)

        @pl.when(seg > 0)
        def _():
            wait_bytes(halo.at[l], hr.at[l])

        @pl.when(seg == 0)
        def _():
            halo[l] = jnp.zeros((16, CH), BF16)

        fbuf[pl.ds(0, 16), :] = halo[l].astype(F32)
        conv_rows(l, 0, 16)

        low64 = low[0:64]
        for j in range(NCH):
            cj = pl.ds(128 * j, 128)
            left = jnp.concatenate([bt * tail[2 * j : 2 * j + 1], bt * tail[2 * j + 1 : 2 * j + 2]], axis=0)
            both = jnp.dot(left.astype(BF16), inp[:, cj], preferred_element_type=F32)
            st = jnp.where(low64, both[0:64], both[64:128]).astype(BF16)
            for q in range(NX):
                lout[l, q, :, cj] = st[16 * q : 16 * q + 16]
        for d in (2, 1, 3):
            xd = (x + d) % NX
            remote(
                lout.at[l, xd], lrecv.at[l, x], xs.at[l, 0], xr.at[l, 0], phase, z * NX + xd
            ).start()
        lrecv[l, x] = lout[l, x]

        @pl.when(l == 0)
        def _():
            weights_2(1)

        for j in range(NCH):
            cj = pl.ds(128 * j, 128)
            v = inp[:, cj]
            vf = v.astype(F32)
            right = jnp.concatenate([jnp.where(low, vf, 0.0), jnp.where(low, 0.0, vf)], axis=0).astype(BF16)
            intra = jnp.dot(wts[j], right, preferred_element_type=F32)
            m0[:, cj] = intra + ppb[l, pl.ds(48 + j, 1), :] * vf

        wait_bytes(grecv.at[l, pl.ds(0, 3)], xr.at[l, 1])
        wait_bytes(lrecv.at[l, pl.ds(0, 3)], xr.at[l, 0])
        p1 = grecv[l, 0]
        p2 = p1 * grecv[l, 1]
        p3 = p2 * grecv[l, 2]
        ggout[l] = p3 * grecv[l, 3]
        ga = grecv[l, 1]
        gb = grecv[l, 2]
        gc = grecv[l, 3]
        for j in range(NCH):
            cj = pl.ds(128 * j, 128)
            r1 = lrecv[l, 0, :, cj].astype(F32)
            r2 = lrecv[l, 1, :, cj].astype(F32) + ga[j : j + 1] * r1
            r3 = lrecv[l, 2, :, cj].astype(F32) + gb[j : j + 1] * r2
            rt = lrecv[l, 3, :, cj].astype(F32) + gc[j : j + 1] * r3
            rb[0, :, cj] = r1
            rb[1, :, cj] = r2
            rb[2, :, cj] = r3
            tout[l, :, cj] = rt.astype(BF16)
        for d in range(REACH, 0, -1):

            @pl.when(z + d < nz)
            def _(d=d):
                to = (z + d) * NX + x
                remote(
                    ggout.at[l], ggrecv.at[l, d - 1], zs.at[l, REACH + d - 1], zr.at[l, REACH + d - 1], phase, to
                ).start()
                remote(tout.at[l], trecv.at[l, d - 1], zs.at[l, d - 1], zr.at[l, d - 1], phase, to).start()

        n = l + 1

        @pl.when(n < LAYERS)
        def _():
            weights_1(n + 1)
            weights_3(n)
            a = product(wbuf[l], ubuf[l + 1])
            for g in range(GROUPS):
                bcuo[n, g] = rows_of(a, g)
                suo[n, g] = a[512 + 16 * g : 528 + 16 * g]
            bcu[n, y] = bcuo[n, y]
            su[n, y] = suo[n, y]
            push_rows(n, 0, bcuo, bcu, suo, su)

        for d in range(1, REACH + 1):

            @pl.when(z >= d)
            def _(d=d):
                wait_bytes(ggrecv.at[l, d - 1], zr.at[l, REACH + d - 1])
                wait_bytes(trecv.at[l, d - 1], zr.at[l, d - 1])

            @pl.when(z < d)
            def _(d=d):
                ggrecv[l, d - 1] = jnp.zeros((8, 128), F32)
                trecv[l, d - 1] = jnp.zeros((16, CH), BF16)

        for j in range(NCH):
            cj = pl.ds(128 * j, 128)
            e = trecv[l, 3, :, cj].astype(F32)
            for d in (2, 1, 0):
                e = trecv[l, d, :, cj].astype(F32) + ggrecv[l, d, pl.ds(j, 1), :] * e
            eout[l, 0, :, cj] = e.astype(BF16)
            eout[l, 1, :, cj] = (rb[0, :, cj] + p1[j : j + 1] * e).astype(BF16)
            eout[l, 2, :, cj] = (rb[1, :, cj] + p2[j : j + 1] * e).astype(BF16)
            eout[l, 3, :, cj] = (rb[2, :, cj] + p3[j : j + 1] * e).astype(BF16)
        for d in (2, 1, 3):
            xd = (x + d) % NX
            remote(
                eout.at[l, xd], ent.at[l, x], xs.at[l, 2], xr.at[l, 2], phase, z * NX + xd
            ).start()
        ent[l, x] = eout[l, x]

        wait_bytes(ent.at[l, pl.ds(0, 3)], xr.at[l, 2])
        sq = jnp.zeros((T, 128), F32)
        for j in range(NCH):
            cj = pl.ds(128 * j, 128)
            part = jnp.dot(cs, ent[l, :, :, cj].reshape(STATE, 128), preferred_element_type=F32)
            mixed = m0[:, cj] + part * gx[:, cj]
            sq = sq + mixed * mixed
            scaled = ppb[l, pl.ds(40 + j, 1), :] * mixed
            gm[:, cj] = scaled
            gmb[:, cj] = scaled.astype(BF16)
        sq_row = jnp.broadcast_to(jnp.sum(jnp.transpose(sq), axis=0, keepdims=True), (8, T))
        for g in range(GROUPS):
            smo[n, g, 16:24] = sq_row

        @pl.when(n < LAYERS)
        def _():
            a = product(wbuf[l], gmb[...])
            for g in range(GROUPS):
                bcmo[n, g] = rows_of(a, g)
                smo[n, g, 0:16] = a[512 + 16 * g : 528 + 16 * g]
            bcm[n, y] = bcmo[n, y]
            sm[n, y] = smo[n, y]
            push_rows(n, 2, bcmo, bcm, smo, sm)

        @pl.when(n == LAYERS)
        def _():
            for g in range(GROUPS):
                smo[n, g, 0:16] = jnp.zeros((16, 128), F32)
            sm[n, y] = smo[n, y]
            for dy in (2, 1, 3):
                yd = (y + dy) % NY
                remote(
                    smo.at[n, yd], sm.at[n, y], ys.at[n, 3], yr.at[n, 3], yd * NC + c, seg
                ).start()

        weights_2(n + 1)
        return carry

    lax.fori_loop(0, LAYERS, layer, 0)

    wait_square(LAYERS)
    inv8 = total_square(LAYERS)
    new_tokens(LAYERS, jnp.transpose(jnp.broadcast_to(inv8[0:1], (T, T))))
    send_out(LAYERS)

    def drain(l, carry):
        n = l + 1

        @pl.when(n < LAYERS)
        def _():
            wait_bytes(bcuo.at[n, pl.ds(0, 3)], ys.at[n, 0])
            wait_bytes(suo.at[n, pl.ds(0, 3)], ys.at[n, 1])
            wait_bytes(bcmo.at[n, pl.ds(0, 3)], ys.at[n, 2])

        wait_bytes(smo.at[n, pl.ds(0, 3)], ys.at[n, 3])
        wait_bytes(ubuf.at[n + 1], outs.at[n])
        wait_bytes(lout.at[l, pl.ds(0, 3)], xs.at[l, 0])
        wait_bytes(grecv.at[l, pl.ds(0, 3)], xs.at[l, 1])
        wait_bytes(eout.at[l, pl.ds(0, 3)], xs.at[l, 2])
        for d in range(1, REACH + 1):

            @pl.when(z + d < nz)
            def _(d=d):
                wait_bytes(ggout.at[l], zs.at[l, REACH + d - 1])
                wait_bytes(tout.at[l], zs.at[l, d - 1])

        @pl.when(seg < nseg - 1)
        def _():
            wait_bytes(halo.at[l], hs.at[l])

        @pl.when(relays(n))
        def _():
            wait_bytes(wbuf.at[l], wrs.at[n])
            for i, rows in enumerate((WPART, WPART, WHALF, WPART - WHALF)):
                wait_bytes(part(n, x, 0, rows), wxs.at[n, i])

        @pl.when(phase != l)
        def _():
            wait_bytes(ubuf.at[0], outr.at[l])
            wait_bytes(ppb.at[l], ppsem.at[l])

        return carry

    lax.fori_loop(0, LAYERS, drain, 0)

    @pl.when(phase > 0)
    def _():
        for dy in range(1, NY):
            wait_bytes(part(1, x, 0, WPART), wss.at[(y + dy) % NY])
        wait_bytes(wbuf.at[0], wss.at[y])

    @pl.when(phase == 0)
    def _():
        for p in range(1, NY * NC):
            wait_bytes(bcuo.at[0, 0], p0s.at[p, 0])
            wait_bytes(suo.at[0, 0], p0s.at[p, 1])

    @pl.when(seg < nseg - 1)
    def _():
        wait_bytes(idsrc, idsem.at[0])


def body(
    stream, doc_ids, in_proj, conv_weight, conv_bias, decay_log, step_bias, skip_gain, norm_gain
):
    nseg = lax.axis_size("seg")
    nz = nseg // NX

    vmem = pltpu.VMEM
    dma = pltpu.SemaphoreType.DMA
    n1 = LAYERS + 1
    return pl.pallas_call(
        functools.partial(kernel, nz),
        out_shape=jax.ShapeDtypeStruct((1, MICRO, T, CH * GROUPS), BF16),
        in_specs=[
            pl.BlockSpec(memory_space=pl.ANY),
            pl.BlockSpec(memory_space=pltpu.VMEM),
            pl.BlockSpec(memory_space=pl.ANY),
        ]
        + [pl.BlockSpec(memory_space=pltpu.VMEM)] * 6,
        out_specs=pl.BlockSpec(memory_space=pl.ANY),
        scratch_shapes=[
            vmem((LAYERS - 1, PROJ, CH), BF16),
            vmem((PROJ, CH * GROUPS), BF16),
            vmem((MICRO, T, CH * GROUPS), BF16),
            vmem((LAYERS + 2, T, CH), BF16),
            vmem((T, CH), F32),
            vmem((T, CH), BF16),
            vmem((GROUPS, 88, 128), F32),
            vmem((HEADS, 128), F32),
            vmem((PROJ, MICRO * T), F32),
            vmem((LAYERS, 88, 128), F32),
            vmem((8, T), jnp.int32),
            vmem((8, T), jnp.int32),
            vmem((KERNEL, T, T), F32),
            vmem((LAYERS, 16, CH), BF16),
            vmem((T + 16, CH), F32),
            vmem((T, CH), BF16),
            vmem((NCH, T, 256), BF16),
            vmem((n1, NY, T, 128), BF16),
            vmem((n1, NY, T, 128), BF16),
            vmem((n1, NY, T, 128), BF16),
            vmem((n1, NY, T, 128), BF16),
            vmem((n1, NY, 16, 128), F32),
            vmem((n1, NY, 24, 128), F32),
            vmem((n1, NY, 16, 128), F32),
            vmem((n1, NY, 24, 128), F32),
            vmem((2, 16, 128), F32),
            vmem((LAYERS, NX, 16, CH), BF16),
            vmem((LAYERS, NX, 16, CH), BF16),
            vmem((LAYERS, 8, 128), F32),
            vmem((LAYERS, NX, 8, 128), F32),
            vmem((LAYERS, 16, CH), BF16),
            vmem((LAYERS, 8, 128), F32),
            vmem((LAYERS, REACH, 16, CH), BF16),
            vmem((LAYERS, REACH, 8, 128), F32),
            vmem((3, 16, CH), F32),
            vmem((LAYERS, NX, 16, CH), BF16),
            vmem((LAYERS, NX, 16, CH), BF16),
            vmem((T, CH), F32),
            vmem((T, CH), F32),
            dma((n1, 4)),
            dma((n1, 4)),
            dma((NY * NC, 2)),
            dma((LAYERS, 3)),
            dma((LAYERS, 3)),
            dma((LAYERS, 2 * REACH)),
            dma((LAYERS, 2 * REACH)),
            dma((LAYERS,)),
            dma((LAYERS,)),
            dma((LAYERS, 7)),
            dma((NY,)),
            dma((LAYERS,)),
            dma((LAYERS, 4)),
            dma((NY * NC,)),
            dma((NY * NC,)),
            dma((n1,)),
            dma((2,)),
            dma((4,)),
        ],
        compiler_params=pltpu.CompilerParams(
            collective_id=0, has_side_effects=True, vmem_limit_bytes=60 * 1024 * 1024
        ),
    )(
        stream,
        doc_ids,
        jnp.swapaxes(in_proj, 1, 2),
        conv_weight,
        conv_bias,
        decay_log,
        step_bias,
        skip_gain,
        norm_gain,
    )


def solution(mesh):
    placed = (
        P(None, "seg", None),
        P(None, "seg"),
        P("phase", None, None),
        P("phase", None, None),
        P("phase", None),
        P("phase", None),
        P("phase", None),
        P("phase", None),
        P("phase", None),
    )
    return jax.shard_map(
        body, mesh=mesh, in_specs=placed, out_specs=P("phase", None, "seg", None), check_vma=False
    )
```

```python
import functools

import jax
import jax.numpy as jnp
from jax import lax
from jax.experimental import pallas as pl
from jax.experimental.pallas import tpu as pltpu
from jax.sharding import PartitionSpec as P

NY = 4
NC = 2
NX = 4
LAYERS = 8
HEADS = 64
HEAD_DIM = 64
STATE = 64
GROUPS = 4
KERNEL = 4
MICRO = 2
T = 128
CH = 1024
PER = 16
NCH = 8
REACH = 4
PROJ = 576
WPART = 144
WHALF = 80
MESH = pl.DeviceIdType.MESH
F32 = jnp.float32
BF16 = jnp.bfloat16


def wait_bytes(ref, sem):
    pltpu.make_async_copy(ref, ref, sem).wait()


def kernel(
    nz,
    stream_ref,
    ids_ref,
    proj_ref,
    convw_ref,
    convb_ref,
    decay_ref,
    stepb_ref,
    skip_ref,
    norm_ref,
    out_ref,
    wbuf,
    w0,
    strm,
    ubuf,
    gm,
    gmb,
    pps,
    pph,
    p0,
    ppb,
    idsrc,
    idh,
    msk,
    halo,
    fbuf,
    inp,
    wts,
    bcu,
    bcm,
    bcuo,
    bcmo,
    su,
    sm,
    suo,
    smo,
    sg,
    lout,
    lrecv,
    gout,
    grecv,
    tout,
    ggout,
    trecv,
    ggrecv,
    rb,
    eout,
    ent,
    m0,
    gx,
    yr,
    ys,
    p0s,
    xr,
    xs,
    zr,
    zs,
    hr,
    hs,
    wr,
    wss,
    wrs,
    wxs,
    ppsem,
    outr,
    outs,
    idsem,
    loc,
):
    phase = lax.axis_index("phase")
    seg = lax.axis_index("seg")
    nseg = nz * NX
    y = phase // NC
    c = phase % NC
    z = seg // NX
    x = seg % NX

    def remote(src, dst, ssem, rsem, p, s):
        return pltpu.make_async_remote_copy(
            src_ref=src,
            dst_ref=dst,
            send_sem=ssem,
            recv_sem=rsem,
            device_id=(p, s),
            device_id_type=MESH,
        )

    barrier = pltpu.get_barrier_semaphore()
    count = 0
    for d in range(1, NY * NC):
        pl.semaphore_signal(barrier, inc=1, device_id=((phase + d) % (NY * NC), seg), device_id_type=MESH)
        count += 1
    for d in range(1, NX):
        pl.semaphore_signal(
            barrier, inc=1, device_id=(phase, z * NX + (x + d) % NX), device_id_type=MESH
        )
        count += 1
    for d in range(1, nz):
        pl.semaphore_signal(
            barrier, inc=1, device_id=(phase, ((z + d) % nz) * NX + x), device_id_type=MESH
        )
        count += 1
    for d in (1, nseg - 1):
        pl.semaphore_signal(barrier, inc=1, device_id=(phase, (seg + d) % nseg), device_id_type=MESH)
        count += 1

    cp_u = pltpu.make_async_copy(
        stream_ref.at[c, :, pl.ds(pl.multiple_of(y * CH, CH), CH)], ubuf.at[0], loc.at[0]
    )
    cp_u.start()
    def quarter(g):
        return proj_ref.at[0, :, pl.ds(pl.multiple_of(g * CH, CH), CH)]

    cp_w0 = pltpu.make_async_copy(proj_ref.at[0], w0, loc.at[1])
    cp_s0 = pltpu.make_async_copy(stream_ref, strm, loc.at[3])

    @pl.when(phase == 0)
    def _():
        cp_w0.start()
        cp_s0.start()

    @pl.when(phase > 0)
    def _():
        pltpu.make_async_copy(quarter(y), wbuf.at[phase - 1], loc.at[2]).start()

    low8 = lax.broadcasted_iota(jnp.int32, (8, 128), 1) < 64
    for g in range(GROUPS):
        for j in range(NCH):
            cj = pl.ds(CH * g + 128 * j, 128)
            for k in range(KERNEL):
                pps[g, pl.ds(8 * k + j, 1), :] = convw_ref[0, pl.ds(k, 1), cj]
            pps[g, pl.ds(32 + j, 1), :] = convb_ref[:, cj]
            pps[g, pl.ds(40 + j, 1), :] = norm_ref[:, cj]

    def per_head(ref):
        return jnp.transpose(jnp.broadcast_to(ref[...], (128, HEADS)))

    pph[...] = per_head(skip_ref)
    decay_rows = per_head(decay_ref)
    stepb_rows = per_head(stepb_ref)
    for g in range(GROUPS):
        pps[g, 48:56] = jnp.where(
            low8, pph[pl.ds(PER * g, 8, stride=2), :], pph[pl.ds(PER * g + 1, 8, stride=2), :]
        )
        pps[g, 56:72] = decay_rows[PER * g : PER * g + PER]
        pps[g, 72:88] = stepb_rows[PER * g : PER * g + PER]
    ppb[phase] = pps[y]

    pl.semaphore_wait(barrier, count)

    idsrc[...] = jnp.broadcast_to(ids_ref[pl.ds(c, 1), :], (8, T))

    @pl.when(seg < nseg - 1)
    def _():
        remote(idsrc, idh, idsem.at[0], idsem.at[1], phase, seg + 1).start()

    @pl.when(seg == 0)
    def _():
        idh[...] = jnp.full((8, T), -1, jnp.int32)

    def send_params():
        for d in range(1, NY * NC):
            p = (phase + d) % (NY * NC)
            remote(pps.at[p // NC], ppb.at[phase], ppsem.at[p], wr.at[phase, 6], p, seg).start()

    def part(n, i, r0, rows):
        return wbuf.at[n - 1, pl.ds(pl.multiple_of(i * WPART + r0, 16), rows), :]

    def send_weights():
        rows = pl.ds(pl.multiple_of(x * WPART, 16), WPART)
        for dy in (2, 1, 3):
            yd = (y + dy) % NY
            remote(
                proj_ref.at[0, rows, pl.ds(pl.multiple_of(yd * CH, CH), CH)],
                part(phase, x, 0, WPART),
                wss.at[yd],
                wr.at[phase, 0],
                yd * NC + c,
                seg,
            ).start()
        remote(quarter(y), wbuf.at[phase - 1], wss.at[y], wr.at[phase, 5], y * NC + 1 - c, seg).start()

    def relays(n):
        return (n < LAYERS) & (c == n % NC) & (y != n // NC)

    right = z * NX + (x + 1) % NX
    left = z * NX + (x + NX - 1) % NX

    def weights_1(n):
        @pl.when(relays(n))
        def _():
            mine = part(n, x, 0, WPART)
            wait_bytes(mine, wr.at[n, 0])
            remote(mine, mine, wxs.at[n, 0], wr.at[n, 1], phase, right).start()
            remote(mine, mine, wxs.at[n, 1], wr.at[n, 2], phase, left).start()

    def weights_2(n):
        @pl.when(relays(n))
        def _():
            wait_bytes(part(n, x, 0, WPART), wr.at[n, 1])
            first = part(n, (x + NX - 1) % NX, 0, WHALF)
            remote(first, first, wxs.at[n, 2], wr.at[n, 3], phase, right).start()
            wait_bytes(part(n, x, 0, WPART), wr.at[n, 2])
            last = part(n, (x + 1) % NX, WHALF, WPART - WHALF)
            remote(last, last, wxs.at[n, 3], wr.at[n, 4], phase, left).start()

    def weights_3(n):
        @pl.when(relays(n))
        def _():
            wait_bytes(part(n, x, 0, WHALF), wr.at[n, 3])
            wait_bytes(part(n, x, 0, WPART - WHALF), wr.at[n, 4])
            whole = wbuf.at[n - 1]
            remote(whole, whole, wrs.at[n], wr.at[n, 5], y * NC + 1 - c, seg).start()

        @pl.when((n < LAYERS) & (c != n % NC))
        def _():
            wait_bytes(wbuf.at[n - 1], wr.at[n, 5])

    lane = lax.broadcasted_iota(jnp.int32, (T, 128), 1)
    low = lane < 64

    def product(w, a):
        return lax.dot_general(w, a, (((1,), (1,)), ((), ())), preferred_element_type=F32)

    def rows_of(a, g):
        return jnp.concatenate(
            [a[64 * g : 64 * g + 64], a[256 + 64 * g : 320 + 64 * g]], axis=0
        ).astype(BF16)

    @pl.when(phase == 0)
    def _():
        send_params()
        cp_w0.wait()
        cp_s0.wait()
        both = strm[...].reshape(MICRO * T, CH * GROUPS)
        for r in range(4):
            rr = pl.ds(WPART * r, WPART)
            p0[rr, :] = product(w0[rr, :], both)
        for m in range(MICRO):
            at = LAYERS * m
            cm = pl.ds(T * m, T)
            for g in range(GROUPS):
                bcuo[at, g, 0:64] = p0[pl.ds(64 * g, 64), cm].astype(BF16)
                bcuo[at, g, 64:128] = p0[pl.ds(256 + 64 * g, 64), cm].astype(BF16)
                suo[at, g] = p0[pl.ds(512 + 16 * g, 16), cm]
            for g in (2, 1, 3, 0):
                p = g * NC + m
                if p > 0:
                    remote(bcuo.at[at, g], bcu.at[0, 0], p0s.at[p, 0], yr.at[0, 0], p, seg).start()
                    remote(suo.at[at, g], su.at[0, 0], p0s.at[p, 1], yr.at[0, 1], p, seg).start()
        bcu[0, 0] = bcuo[0, 0]
        su[0, 0] = suo[0, 0]

    @pl.when((phase == 1) | (phase == 2))
    def _():
        send_params()
        send_weights()

    cp_u.wait()

    @pl.when(phase > 0)
    def _():
        pltpu.make_async_copy(quarter(y), wbuf.at[phase - 1], loc.at[2]).wait()

    bcm[0] = jnp.zeros((NY, T, 128), BF16)
    sm[0] = jnp.zeros((NY, 24, 128), F32)
    for s in range(1, NY):
        bcu[0, s] = jnp.zeros((T, 128), BF16)
        su[0, s] = jnp.zeros((16, 128), F32)
    gm[...] = jnp.zeros((T, CH), F32)

    @pl.when(seg > 0)
    def _():
        wait_bytes(idh, idsem.at[1])

    own_row = idsrc[...].astype(F32)
    prior_row = idh[...].astype(F32)
    lane8 = lax.broadcasted_iota(jnp.int32, (8, T), 1)
    row_rep = jnp.broadcast_to(own_row[0:1], (T, T))
    col_rep = jnp.transpose(row_rep)
    t_at = lax.broadcasted_iota(jnp.int32, (T, T), 0)
    msk[0] = jnp.where((row_rep == col_rep) & (t_at >= lane), 1.0, 0.0)
    for k in range(1, KERNEL):
        behind = jnp.where(lane8 < k, pltpu.roll(prior_row, k, 1), pltpu.roll(own_row, k, 1))
        same = jnp.where(behind == own_row, 1.0, 0.0)
        msk[k] = jnp.transpose(jnp.broadcast_to(same[0:1], (T, T)))
    prior_last = jnp.broadcast_to(prior_row[:, T - 1 : T], (8, T))
    own_last = jnp.broadcast_to(own_row[:, T - 1 : T], (8, T))
    sg[1, 0:8] = jnp.where(own_row == prior_last, 1.0, 0.0)
    sg[1, 8:16] = jnp.where(own_row == own_last, 1.0, 0.0)
    sum_up = jnp.where(t_at <= lane, 1.0, 0.0)
    weights_1(1)

    def total_square(lx):
        s = sm[lx, 0, 16:24] + sm[lx, 1, 16:24] + sm[lx, 2, 16:24] + sm[lx, 3, 16:24]
        return lax.rsqrt(s * (1.0 / (CH * GROUPS)) + 1e-05)

    def new_tokens(lx, inv_rep):
        for j in range(NCH):
            cj = pl.ds(128 * j, 128)
            u = ubuf[lx, :, cj].astype(F32) + gm[:, cj] * inv_rep
            ub = u.astype(BF16)
            ubuf[lx + 1, :, cj] = ub
            fbuf[pl.ds(16, T), cj] = ub.astype(F32)

    def send_out(lx):
        there = out_ref.at[0, c, :, pl.ds(pl.multiple_of(y * CH, CH), CH)]

        @pl.when(phase == lx - 1)
        def _():
            pltpu.make_async_copy(ubuf.at[lx + 1], there, outs.at[lx]).start()

        @pl.when(phase != lx - 1)
        def _():
            remote(ubuf.at[lx + 1], there, outs.at[lx], outr.at[phase], lx - 1, seg).start()

    def wait_square(lx):
        wait_bytes(sm.at[lx, pl.ds(0, 3)], yr.at[lx, 3])

    def push(lx, kind, outbuf, inbuf):
        for dy in (2, 1, 3):
            yd = (y + dy) % NY
            remote(
                outbuf.at[lx, yd], inbuf.at[lx, y], ys.at[lx, kind], yr.at[lx, kind], yd * NC + c, seg
            ).start()
        inbuf[lx, y] = outbuf[lx, y]

    def conv_rows(l, r0, n):
        for j in range(NCH):
            cj = pl.ds(128 * j, 128)
            acc = fbuf[pl.ds(16 + r0, n), cj] * ppb[l, pl.ds(24 + j, 1), :] + ppb[l, pl.ds(32 + j, 1), :]
            for k in range(1, KERNEL):
                tap = ppb[l, pl.ds(8 * (3 - k) + j, 1), :]
                acc = acc + (fbuf[pl.ds(16 + r0 - k, n), cj] * msk[k, pl.ds(r0, n), :]) * tap
            inp[pl.ds(r0, n), cj] = (acc * (1.0 / (1.0 + jnp.exp(-acc)))).astype(BF16)

    def layer(l, carry):
        @pl.when((l == 0) & (phase > 0))
        def _():
            wait_bytes(su.at[0, 0], yr.at[0, 1])

        @pl.when(l > 0)
        def _():
            wait_bytes(su.at[l, pl.ds(0, 3)], yr.at[l, 1])
            wait_square(l)

        inv8 = total_square(l)
        inv_rep = jnp.transpose(jnp.broadcast_to(inv8[0:1], (T, T)))
        new_tokens(l, inv_rep)

        @pl.when(seg < nseg - 1)
        def _():
            remote(
                ubuf.at[l + 1, pl.ds(T - 16, 16), :], halo.at[l], hs.at[l], hr.at[l], phase, seg + 1
            ).start()

        weights_2(l + 1)

        @pl.when(phase != l)
        def _():
            wait_bytes(ppb.at[l], wr.at[l, 6])

        s_u = su[l, 0] + su[l, 1] + su[l, 2] + su[l, 3]
        s_m = sm[l, 0, 0:16] + sm[l, 1, 0:16] + sm[l, 2, 0:16] + sm[l, 3, 0:16]
        pre = s_u + inv8[0:1] * s_m + ppb[l, 72:88]
        step = jnp.maximum(pre, 0.0) + jnp.log1p(jnp.exp(-jnp.abs(pre)))
        log_decay = -jnp.exp(ppb[l, 56:72]) * step
        run = jnp.dot(log_decay, sum_up, preferred_element_type=F32, precision=lax.Precision.HIGHEST)
        goes_on = sg[1, 0:1]
        is_last = sg[1, 8:9]
        cgain = jnp.exp(run) * goes_on
        tail = jnp.exp(jnp.broadcast_to(run[:, T - 1 : T], (PER, T)) - run) * is_last * step
        sg[0] = jnp.broadcast_to(cgain[:, T - 1 : T], (PER, T))
        gain8 = jnp.where(
            lane8 < 64, sg[0, pl.ds(0, 8, stride=2), :], sg[0, pl.ds(1, 8, stride=2), :]
        )
        gout[l] = gain8
        grecv[l, x] = gain8
        for d in range(1, NX):
            xd = (x + d) % NX
            remote(gout.at[l], grecv.at[l, x], xs.at[l, 1], xr.at[l, 1], phase, z * NX + xd).start()

        conv_rows(l, 16, T - 16)

        @pl.when((l == 0) & (phase > 0))
        def _():
            wait_bytes(bcu.at[0, 0], yr.at[0, 0])

        @pl.when(l > 0)
        def _():
            wait_bytes(bcu.at[l, pl.ds(0, 3)], yr.at[l, 0])
            wait_bytes(bcm.at[l, pl.ds(0, 3)], yr.at[l, 2])

        bc_u = (
            bcu[l, 0].astype(F32) + bcu[l, 1].astype(F32) + bcu[l, 2].astype(F32) + bcu[l, 3].astype(F32)
        )
        bc_m = (
            bcm[l, 0].astype(F32) + bcm[l, 1].astype(F32) + bcm[l, 2].astype(F32) + bcm[l, 3].astype(F32)
        )
        bc = (bc_u + inv8[0:1] * bc_m).astype(BF16)
        bt = bc[0:64].astype(F32)
        cs = jnp.transpose(bc[64:128].astype(F32)).astype(BF16)
        scores = jnp.dot(cs, bc[0:64], preferred_element_type=F32)
        scores = scores * msk[0]

        @pl.when(seg > 0)
        def _():
            wait_bytes(halo.at[l], hr.at[l])

        @pl.when(seg == 0)
        def _():
            halo[l] = jnp.zeros((16, CH), BF16)

        fbuf[pl.ds(0, 16), :] = halo[l].astype(F32)
        conv_rows(l, 0, 16)

        low64 = low[0:64]
        for j in range(NCH):
            cj = pl.ds(128 * j, 128)
            left = jnp.concatenate([bt * tail[2 * j : 2 * j + 1], bt * tail[2 * j + 1 : 2 * j + 2]], axis=0)
            both = jnp.dot(left.astype(BF16), inp[:, cj], preferred_element_type=F32)
            st = jnp.where(low64, both[0:64], both[64:128]).astype(BF16)
            for q in range(NX):
                lout[l, q, :, cj] = st[16 * q : 16 * q + 16]
        for d in (2, 1, 3):
            xd = (x + d) % NX
            remote(
                lout.at[l, xd], lrecv.at[l, x], xs.at[l, 0], xr.at[l, 0], phase, z * NX + xd
            ).start()
        lrecv[l, x] = lout[l, x]

        @pl.when(l > 0)
        def _():
            send_out(l)

        @pl.when(phase == l + 3)
        def _():
            send_params()
            send_weights()

        cols = jnp.transpose(jnp.concatenate([run, cgain, jnp.zeros((T - 2 * PER, T), F32)], axis=0))
        for j in range(NCH):
            for i in range(2):
                h = 2 * j + i
                gap = jnp.broadcast_to(cols[:, h : h + 1], (T, T)) - run[h : h + 1]
                w = scores * (jnp.exp(jnp.minimum(gap, 0.0)) * step[h : h + 1])
                wts[j, :, pl.ds(128 * i, 128)] = w.astype(BF16)

        for j in range(NCH):
            cj = pl.ds(128 * j, 128)
            v = inp[:, cj]
            vf = v.astype(F32)
            right = jnp.concatenate([jnp.where(low, vf, 0.0), jnp.where(low, 0.0, vf)], axis=0).astype(BF16)
            intra = jnp.dot(wts[j], right, preferred_element_type=F32)
            m0[:, cj] = intra + ppb[l, pl.ds(48 + j, 1), :] * vf

        wait_bytes(grecv.at[l, pl.ds(0, 3)], xr.at[l, 1])
        wait_bytes(lrecv.at[l, pl.ds(0, 3)], xr.at[l, 0])
        p1 = grecv[l, 0]
        p2 = p1 * grecv[l, 1]
        p3 = p2 * grecv[l, 2]
        ggout[l] = p3 * grecv[l, 3]
        ga = grecv[l, 1]
        gb = grecv[l, 2]
        gc = grecv[l, 3]
        for j in range(NCH):
            cj = pl.ds(128 * j, 128)
            r1 = lrecv[l, 0, :, cj].astype(F32)
            r2 = lrecv[l, 1, :, cj].astype(F32) + ga[j : j + 1] * r1
            r3 = lrecv[l, 2, :, cj].astype(F32) + gb[j : j + 1] * r2
            rt = lrecv[l, 3, :, cj].astype(F32) + gc[j : j + 1] * r3
            rb[0, :, cj] = r1
            rb[1, :, cj] = r2
            rb[2, :, cj] = r3
            tout[l, :, cj] = rt.astype(BF16)
        for d in range(1, REACH + 1):

            @pl.when(z + d < nz)
            def _(d=d):
                to = (z + d) * NX + x
                remote(
                    ggout.at[l], ggrecv.at[l, d - 1], zs.at[l, REACH + d - 1], zr.at[l, REACH + d - 1], phase, to
                ).start()
                remote(tout.at[l], trecv.at[l, d - 1], zs.at[l, d - 1], zr.at[l, d - 1], phase, to).start()

        n = l + 1

        @pl.when(n < LAYERS)
        def _():
            weights_3(n)
            a = product(wbuf[l], ubuf[l + 1])
            for g in range(GROUPS):
                bcuo[n, g] = rows_of(a, g)
                suo[n, g] = a[512 + 16 * g : 528 + 16 * g]
            push(n, 1, suo, su)
            push(n, 0, bcuo, bcu)

        for d in range(1, REACH + 1):

            @pl.when(z >= d)
            def _(d=d):
                wait_bytes(ggrecv.at[l, d - 1], zr.at[l, REACH + d - 1])
                wait_bytes(trecv.at[l, d - 1], zr.at[l, d - 1])

            @pl.when(z < d)
            def _(d=d):
                ggrecv[l, d - 1] = jnp.zeros((8, 128), F32)
                trecv[l, d - 1] = jnp.zeros((16, CH), BF16)

        for j in range(NCH):
            cj = pl.ds(128 * j, 128)
            e = trecv[l, 3, :, cj].astype(F32)
            for d in (2, 1, 0):
                e = trecv[l, d, :, cj].astype(F32) + ggrecv[l, d, pl.ds(j, 1), :] * e
            eout[l, 0, :, cj] = e.astype(BF16)
            eout[l, 1, :, cj] = (rb[0, :, cj] + p1[j : j + 1] * e).astype(BF16)
            eout[l, 2, :, cj] = (rb[1, :, cj] + p2[j : j + 1] * e).astype(BF16)
            eout[l, 3, :, cj] = (rb[2, :, cj] + p3[j : j + 1] * e).astype(BF16)
        for d in (2, 1, 3):
            xd = (x + d) % NX
            remote(
                eout.at[l, xd], ent.at[l, x], xs.at[l, 2], xr.at[l, 2], phase, z * NX + xd
            ).start()
        ent[l, x] = eout[l, x]

        for j in range(NCH):
            g0 = jnp.broadcast_to(cols[:, PER + 2 * j : PER + 2 * j + 1], (T, T))
            g1 = jnp.broadcast_to(cols[:, PER + 2 * j + 1 : PER + 2 * j + 2], (T, T))
            gx[:, pl.ds(128 * j, 128)] = jnp.where(low, g0, g1)
        wait_bytes(ent.at[l, pl.ds(0, 3)], xr.at[l, 2])
        weights_1(n + 1)
        sq = jnp.zeros((T, 128), F32)
        for j in range(NCH):
            cj = pl.ds(128 * j, 128)
            part = jnp.dot(cs, ent[l, :, :, cj].reshape(STATE, 128), preferred_element_type=F32)
            mixed = m0[:, cj] + part * gx[:, cj]
            sq = sq + mixed * mixed
            scaled = ppb[l, pl.ds(40 + j, 1), :] * mixed
            gm[:, cj] = scaled
            gmb[:, cj] = scaled.astype(BF16)
        sq_row = jnp.broadcast_to(jnp.sum(jnp.transpose(sq), axis=0, keepdims=True), (8, T))
        for g in range(GROUPS):
            smo[n, g, 16:24] = sq_row

        @pl.when(n < LAYERS)
        def _():
            v = gmb[...]
            a = product(wbuf[l, 512:576, :], v)
            for g in range(GROUPS):
                smo[n, g, 0:16] = a[16 * g : 16 * g + 16]
            push(n, 3, smo, sm)
            a = product(wbuf[l, 0:512, :], v)
            for g in range(GROUPS):
                bcmo[n, g] = rows_of(a, g)
            push(n, 2, bcmo, bcm)

        @pl.when(n == LAYERS)
        def _():
            for g in range(GROUPS):
                smo[n, g, 0:16] = jnp.zeros((16, 128), F32)
            push(n, 3, smo, sm)

        return carry

    lax.fori_loop(0, LAYERS, layer, 0)

    wait_square(LAYERS)
    inv8 = total_square(LAYERS)
    new_tokens(LAYERS, jnp.transpose(jnp.broadcast_to(inv8[0:1], (T, T))))
    send_out(LAYERS)

    def drain(l, carry):
        n = l + 1

        @pl.when(n < LAYERS)
        def _():
            wait_bytes(bcuo.at[n, pl.ds(0, 3)], ys.at[n, 0])
            wait_bytes(suo.at[n, pl.ds(0, 3)], ys.at[n, 1])
            wait_bytes(bcmo.at[n, pl.ds(0, 3)], ys.at[n, 2])

        wait_bytes(smo.at[n, pl.ds(0, 3)], ys.at[n, 3])
        wait_bytes(ubuf.at[n + 1], outs.at[n])
        wait_bytes(lout.at[l, pl.ds(0, 3)], xs.at[l, 0])
        wait_bytes(grecv.at[l, pl.ds(0, 3)], xs.at[l, 1])
        wait_bytes(eout.at[l, pl.ds(0, 3)], xs.at[l, 2])
        for d in range(1, REACH + 1):

            @pl.when(z + d < nz)
            def _(d=d):
                wait_bytes(ggout.at[l], zs.at[l, REACH + d - 1])
                wait_bytes(tout.at[l], zs.at[l, d - 1])

        @pl.when(seg < nseg - 1)
        def _():
            wait_bytes(halo.at[l], hs.at[l])

        @pl.when(relays(n))
        def _():
            wait_bytes(wbuf.at[l], wrs.at[n])
            for i, rows in enumerate((WPART, WPART, WHALF, WPART - WHALF)):
                wait_bytes(part(n, x, 0, rows), wxs.at[n, i])

        @pl.when(phase != l)
        def _():
            wait_bytes(ubuf.at[0], outr.at[l])
            wait_bytes(ppb.at[l], ppsem.at[l])

        return carry

    lax.fori_loop(0, LAYERS, drain, 0)

    @pl.when(phase > 0)
    def _():
        for dy in range(1, NY):
            wait_bytes(part(1, x, 0, WPART), wss.at[(y + dy) % NY])
        wait_bytes(wbuf.at[0], wss.at[y])

    @pl.when(phase == 0)
    def _():
        for p in range(1, NY * NC):
            wait_bytes(bcuo.at[0, 0], p0s.at[p, 0])
            wait_bytes(suo.at[0, 0], p0s.at[p, 1])

    @pl.when(seg < nseg - 1)
    def _():
        wait_bytes(idsrc, idsem.at[0])


def body(
    stream, doc_ids, in_proj, conv_weight, conv_bias, decay_log, step_bias, skip_gain, norm_gain
):
    nseg = lax.axis_size("seg")
    nz = nseg // NX

    vmem = pltpu.VMEM
    dma = pltpu.SemaphoreType.DMA
    n1 = LAYERS + 1
    return pl.pallas_call(
        functools.partial(kernel, nz),
        out_shape=jax.ShapeDtypeStruct((1, MICRO, T, CH * GROUPS), BF16),
        in_specs=[
            pl.BlockSpec(memory_space=pl.ANY),
            pl.BlockSpec(memory_space=pltpu.VMEM),
            pl.BlockSpec(memory_space=pl.ANY),
        ]
        + [pl.BlockSpec(memory_space=pltpu.VMEM)] * 6,
        out_specs=pl.BlockSpec(memory_space=pl.ANY),
        scratch_shapes=[
            vmem((LAYERS - 1, PROJ, CH), BF16),
            vmem((PROJ, CH * GROUPS), BF16),
            vmem((MICRO, T, CH * GROUPS), BF16),
            vmem((LAYERS + 2, T, CH), BF16),
            vmem((T, CH), F32),
            vmem((T, CH), BF16),
            vmem((GROUPS, 88, 128), F32),
            vmem((HEADS, 128), F32),
            vmem((PROJ, MICRO * T), F32),
            vmem((LAYERS, 88, 128), F32),
            vmem((8, T), jnp.int32),
            vmem((8, T), jnp.int32),
            vmem((KERNEL, T, T), F32),
            vmem((LAYERS, 16, CH), BF16),
            vmem((T + 16, CH), F32),
            vmem((T, CH), BF16),
            vmem((NCH, T, 256), BF16),
            vmem((n1, NY, T, 128), BF16),
            vmem((n1, NY, T, 128), BF16),
            vmem((n1, NY, T, 128), BF16),
            vmem((n1, NY, T, 128), BF16),
            vmem((n1, NY, 16, 128), F32),
            vmem((n1, NY, 24, 128), F32),
            vmem((n1, NY, 16, 128), F32),
            vmem((n1, NY, 24, 128), F32),
            vmem((2, 16, 128), F32),
            vmem((LAYERS, NX, 16, CH), BF16),
            vmem((LAYERS, NX, 16, CH), BF16),
            vmem((LAYERS, 8, 128), F32),
            vmem((LAYERS, NX, 8, 128), F32),
            vmem((LAYERS, 16, CH), BF16),
            vmem((LAYERS, 8, 128), F32),
            vmem((LAYERS, REACH, 16, CH), BF16),
            vmem((LAYERS, REACH, 8, 128), F32),
            vmem((3, 16, CH), F32),
            vmem((LAYERS, NX, 16, CH), BF16),
            vmem((LAYERS, NX, 16, CH), BF16),
            vmem((T, CH), F32),
            vmem((T, CH), F32),
            dma((n1, 4)),
            dma((n1, 4)),
            dma((NY * NC, 2)),
            dma((LAYERS, 3)),
            dma((LAYERS, 3)),
            dma((LAYERS, 2 * REACH)),
            dma((LAYERS, 2 * REACH)),
            dma((LAYERS,)),
            dma((LAYERS,)),
            dma((LAYERS, 7)),
            dma((NY,)),
            dma((LAYERS,)),
            dma((LAYERS, 4)),
            dma((NY * NC,)),
            dma((NY * NC,)),
            dma((n1,)),
            dma((2,)),
            dma((4,)),
        ],
        compiler_params=pltpu.CompilerParams(
            collective_id=0, has_side_effects=True, vmem_limit_bytes=60 * 1024 * 1024
        ),
    )(
        stream,
        doc_ids,
        jnp.swapaxes(in_proj, 1, 2),
        conv_weight,
        conv_bias,
        decay_log,
        step_bias,
        skip_gain,
        norm_gain,
    )


def solution(mesh):
    placed = (
        P(None, "seg", None),
        P(None, "seg"),
        P("phase", None, None),
        P("phase", None, None),
        P("phase", None),
        P("phase", None),
        P("phase", None),
        P("phase", None),
        P("phase", None),
    )
    return jax.shard_map(
        body, mesh=mesh, in_specs=placed, out_specs=P("phase", None, "seg", None), check_vma=False
    )
```

```python
import functools

import jax
import jax.numpy as jnp
from jax import lax
from jax.experimental import pallas as pl
from jax.experimental.pallas import tpu as pltpu
from jax.sharding import PartitionSpec as P

NY = 4
NC = 2
NX = 4
LAYERS = 8
HEADS = 64
HEAD_DIM = 64
STATE = 64
GROUPS = 4
KERNEL = 4
MICRO = 2
T = 128
CH = 1024
PER = 16
NCH = 8
REACH = 4
PROJ = 576
WPART = 144
WHALF = 80
MESH = pl.DeviceIdType.MESH
F32 = jnp.float32
BF16 = jnp.bfloat16


def wait_bytes(ref, sem):
    pltpu.make_async_copy(ref, ref, sem).wait()


def kernel(
    nz,
    stream_ref,
    ids_ref,
    proj_ref,
    convw_ref,
    convb_ref,
    decay_ref,
    stepb_ref,
    skip_ref,
    norm_ref,
    out_ref,
    wbuf,
    w0,
    strm,
    ubuf,
    gm,
    gmb,
    pps,
    pph,
    p0,
    ppb,
    idsrc,
    idh,
    msk,
    halo,
    fbuf,
    inp,
    wts,
    bcu,
    bm,
    cm,
    bcuo,
    bmo,
    cmo,
    su,
    sm,
    suo,
    smo,
    sg,
    lout,
    lrecv,
    gout,
    grecv,
    tout,
    ggout,
    trecv,
    ggrecv,
    rb,
    eout,
    ent,
    m0,
    gx,
    yr,
    ys,
    p0s,
    xr,
    xs,
    zr,
    zs,
    hr,
    hs,
    wr,
    wss,
    wrs,
    wxs,
    ppsem,
    outr,
    outs,
    idsem,
    loc,
):
    phase = lax.axis_index("phase")
    seg = lax.axis_index("seg")
    nseg = nz * NX
    y = phase // NC
    c = phase % NC
    z = seg // NX
    x = seg % NX

    def remote(src, dst, ssem, rsem, p, s):
        return pltpu.make_async_remote_copy(
            src_ref=src,
            dst_ref=dst,
            send_sem=ssem,
            recv_sem=rsem,
            device_id=(p, s),
            device_id_type=MESH,
        )

    barrier = pltpu.get_barrier_semaphore()
    count = 0
    for d in range(1, NY * NC):
        pl.semaphore_signal(barrier, inc=1, device_id=((phase + d) % (NY * NC), seg), device_id_type=MESH)
        count += 1
    for d in range(1, NX):
        pl.semaphore_signal(
            barrier, inc=1, device_id=(phase, z * NX + (x + d) % NX), device_id_type=MESH
        )
        count += 1
    for d in range(1, nz):
        pl.semaphore_signal(
            barrier, inc=1, device_id=(phase, ((z + d) % nz) * NX + x), device_id_type=MESH
        )
        count += 1
    for d in (1, nseg - 1):
        pl.semaphore_signal(barrier, inc=1, device_id=(phase, (seg + d) % nseg), device_id_type=MESH)
        count += 1

    cp_u = pltpu.make_async_copy(
        stream_ref.at[c, :, pl.ds(pl.multiple_of(y * CH, CH), CH)], ubuf.at[0], loc.at[0]
    )
    cp_u.start()
    def quarter(g):
        return proj_ref.at[0, :, pl.ds(pl.multiple_of(g * CH, CH), CH)]

    cp_w0 = pltpu.make_async_copy(proj_ref.at[0], w0, loc.at[1])
    cp_s0 = pltpu.make_async_copy(stream_ref, strm, loc.at[3])

    @pl.when(phase == 0)
    def _():
        cp_w0.start()
        cp_s0.start()

    @pl.when(phase > 0)
    def _():
        pltpu.make_async_copy(quarter(y), wbuf.at[phase - 1], loc.at[2]).start()

    low8 = lax.broadcasted_iota(jnp.int32, (8, 128), 1) < 64
    for g in range(GROUPS):
        for j in range(NCH):
            cj = pl.ds(CH * g + 128 * j, 128)
            for k in range(KERNEL):
                pps[g, pl.ds(8 * k + j, 1), :] = convw_ref[0, pl.ds(k, 1), cj]
            pps[g, pl.ds(32 + j, 1), :] = convb_ref[:, cj]
            pps[g, pl.ds(40 + j, 1), :] = norm_ref[:, cj]

    def per_head(ref):
        return jnp.transpose(jnp.broadcast_to(ref[...], (128, HEADS)))

    pph[...] = per_head(skip_ref)
    decay_rows = per_head(decay_ref)
    stepb_rows = per_head(stepb_ref)
    for g in range(GROUPS):
        pps[g, 48:56] = jnp.where(
            low8, pph[pl.ds(PER * g, 8, stride=2), :], pph[pl.ds(PER * g + 1, 8, stride=2), :]
        )
        pps[g, 56:72] = decay_rows[PER * g : PER * g + PER]
        pps[g, 72:88] = stepb_rows[PER * g : PER * g + PER]
    ppb[phase] = pps[y]

    pl.semaphore_wait(barrier, count)

    idsrc[...] = jnp.broadcast_to(ids_ref[pl.ds(c, 1), :], (8, T))

    @pl.when(seg < nseg - 1)
    def _():
        remote(idsrc, idh, idsem.at[0], idsem.at[1], phase, seg + 1).start()

    @pl.when(seg == 0)
    def _():
        idh[...] = jnp.full((8, T), -1, jnp.int32)

    def send_params():
        for d in range(1, NY * NC):
            p = (phase + d) % (NY * NC)
            remote(pps.at[p // NC], ppb.at[phase], ppsem.at[p], wr.at[phase, 6], p, seg).start()

    def part(n, i, r0, rows):
        return wbuf.at[n - 1, pl.ds(pl.multiple_of(i * WPART + r0, 16), rows), :]

    def send_weights():
        rows = pl.ds(pl.multiple_of(x * WPART, 16), WPART)
        for dy in (2, 1, 3):
            yd = (y + dy) % NY
            remote(
                proj_ref.at[0, rows, pl.ds(pl.multiple_of(yd * CH, CH), CH)],
                part(phase, x, 0, WPART),
                wss.at[yd],
                wr.at[phase, 0],
                yd * NC + c,
                seg,
            ).start()
        remote(quarter(y), wbuf.at[phase - 1], wss.at[y], wr.at[phase, 5], y * NC + 1 - c, seg).start()

    def relays(n):
        return (n < LAYERS) & (c == n % NC) & (y != n // NC)

    right = z * NX + (x + 1) % NX
    left = z * NX + (x + NX - 1) % NX

    def weights_1(n):
        @pl.when(relays(n))
        def _():
            mine = part(n, x, 0, WPART)
            wait_bytes(mine, wr.at[n, 0])
            remote(mine, mine, wxs.at[n, 0], wr.at[n, 1], phase, right).start()
            remote(mine, mine, wxs.at[n, 1], wr.at[n, 2], phase, left).start()

    def weights_2(n):
        @pl.when(relays(n))
        def _():
            wait_bytes(part(n, x, 0, WPART), wr.at[n, 1])
            first = part(n, (x + NX - 1) % NX, 0, WHALF)
            remote(first, first, wxs.at[n, 2], wr.at[n, 3], phase, right).start()
            wait_bytes(part(n, x, 0, WPART), wr.at[n, 2])
            last = part(n, (x + 1) % NX, WHALF, WPART - WHALF)
            remote(last, last, wxs.at[n, 3], wr.at[n, 4], phase, left).start()

    def weights_3(n):
        @pl.when(relays(n))
        def _():
            wait_bytes(part(n, x, 0, WHALF), wr.at[n, 3])
            wait_bytes(part(n, x, 0, WPART - WHALF), wr.at[n, 4])
            whole = wbuf.at[n - 1]
            remote(whole, whole, wrs.at[n], wr.at[n, 5], y * NC + 1 - c, seg).start()

    def weights_4(n):
        @pl.when((n < LAYERS) & (c != n % NC))
        def _():
            wait_bytes(wbuf.at[n - 1], wr.at[n, 5])

    lane = lax.broadcasted_iota(jnp.int32, (T, 128), 1)
    low = lane < 64

    def product(w, a):
        return lax.dot_general(w, a, (((1,), (1,)), ((), ())), preferred_element_type=F32)

    def rows_of(a, g):
        return jnp.concatenate(
            [a[64 * g : 64 * g + 64], a[256 + 64 * g : 320 + 64 * g]], axis=0
        ).astype(BF16)

    @pl.when(phase == 0)
    def _():
        send_params()
        cp_w0.wait()
        cp_s0.wait()
        for m in range(MICRO):
            at = LAYERS * m
            mine = strm[m]
            for r in range(4):
                rr = pl.ds(WPART * r, WPART)
                p0[rr, :] = product(w0[rr, :], mine)
            for g in range(GROUPS):
                bcuo[at, g, 0:64] = p0[pl.ds(64 * g, 64), :].astype(BF16)
                bcuo[at, g, 64:128] = p0[pl.ds(256 + 64 * g, 64), :].astype(BF16)
                suo[at, g] = p0[pl.ds(512 + 16 * g, 16), :]
            for g in (2, 1, 3, 0):
                p = g * NC + m
                if p > 0:
                    remote(bcuo.at[at, g], bcu.at[0, 0], p0s.at[p, 0], yr.at[0, 0], p, seg).start()
                    remote(suo.at[at, g], su.at[0, 0], p0s.at[p, 1], yr.at[0, 1], p, seg).start()
        bcu[0, 0] = bcuo[0, 0]
        su[0, 0] = suo[0, 0]

    @pl.when((phase >= 1) & (phase <= 3))
    def _():
        send_params()
        send_weights()

    cp_u.wait()

    @pl.when(phase > 0)
    def _():
        pltpu.make_async_copy(quarter(y), wbuf.at[phase - 1], loc.at[2]).wait()

    bm[0] = jnp.zeros((NY, 64, 128), BF16)
    cm[0] = jnp.zeros((NY, 64, 128), BF16)
    sm[0] = jnp.zeros((NY, 24, 128), F32)
    for s in range(1, NY):
        bcu[0, s] = jnp.zeros((T, 128), BF16)
        su[0, s] = jnp.zeros((16, 128), F32)
    gm[...] = jnp.zeros((T, CH), F32)

    @pl.when(seg > 0)
    def _():
        wait_bytes(idh, idsem.at[1])

    own_row = idsrc[...].astype(F32)
    prior_row = idh[...].astype(F32)
    lane8 = lax.broadcasted_iota(jnp.int32, (8, T), 1)
    row_rep = jnp.broadcast_to(own_row[0:1], (T, T))
    col_rep = jnp.transpose(row_rep)
    t_at = lax.broadcasted_iota(jnp.int32, (T, T), 0)
    msk[0] = jnp.where((row_rep == col_rep) & (t_at >= lane), 1.0, 0.0)
    for k in range(1, KERNEL):
        behind = jnp.where(lane8 < k, pltpu.roll(prior_row, k, 1), pltpu.roll(own_row, k, 1))
        same = jnp.where(behind == own_row, 1.0, 0.0)
        msk[k] = jnp.transpose(jnp.broadcast_to(same[0:1], (T, T)))
    prior_last = jnp.broadcast_to(prior_row[:, T - 1 : T], (8, T))
    own_last = jnp.broadcast_to(own_row[:, T - 1 : T], (8, T))
    sg[1, 0:8] = jnp.where(own_row == prior_last, 1.0, 0.0)
    sg[1, 8:16] = jnp.where(own_row == own_last, 1.0, 0.0)
    sum_up = jnp.where(t_at <= lane, 1.0, 0.0)
    weights_1(1)
    weights_1(2)

    def total_square(lx):
        s = sm[lx, 0, 16:24] + sm[lx, 1, 16:24] + sm[lx, 2, 16:24] + sm[lx, 3, 16:24]
        return lax.rsqrt(s * (1.0 / (CH * GROUPS)) + 1e-05)

    def new_tokens(lx, inv_rep):
        for j in range(NCH):
            cj = pl.ds(128 * j, 128)
            u = ubuf[lx, :, cj].astype(F32) + gm[:, cj] * inv_rep
            ub = u.astype(BF16)
            ubuf[lx + 1, :, cj] = ub
            fbuf[pl.ds(16, T), cj] = ub.astype(F32)

    def send_out(lx):
        there = out_ref.at[0, c, :, pl.ds(pl.multiple_of(y * CH, CH), CH)]

        @pl.when(phase == lx - 1)
        def _():
            pltpu.make_async_copy(ubuf.at[lx + 1], there, outs.at[lx]).start()

        @pl.when(phase != lx - 1)
        def _():
            remote(ubuf.at[lx + 1], there, outs.at[lx], outr.at[phase], lx - 1, seg).start()

    def wait_square(lx):
        wait_bytes(sm.at[lx, pl.ds(0, 3)], yr.at[lx, 3])

    def push(lx, kind, outbuf, inbuf):
        for dy in (2, 1, 3):
            yd = (y + dy) % NY
            remote(
                outbuf.at[lx, yd], inbuf.at[lx, y], ys.at[lx, kind], yr.at[lx, kind], yd * NC + c, seg
            ).start()
        inbuf[lx, y] = outbuf[lx, y]

    def conv_rows(l, r0, n):
        for j in range(NCH):
            cj = pl.ds(128 * j, 128)
            acc = fbuf[pl.ds(16 + r0, n), cj] * ppb[l, pl.ds(24 + j, 1), :] + ppb[l, pl.ds(32 + j, 1), :]
            for k in range(1, KERNEL):
                tap = ppb[l, pl.ds(8 * (3 - k) + j, 1), :]
                acc = acc + (fbuf[pl.ds(16 + r0 - k, n), cj] * msk[k, pl.ds(r0, n), :]) * tap
            inp[pl.ds(r0, n), cj] = (acc * (1.0 / (1.0 + jnp.exp(-acc)))).astype(BF16)

    def layer(l, carry):
        @pl.when((l == 0) & (phase > 0))
        def _():
            wait_bytes(su.at[0, 0], yr.at[0, 1])

        @pl.when(l > 0)
        def _():
            wait_bytes(su.at[l, pl.ds(0, 3)], yr.at[l, 1])
            wait_square(l)

        inv8 = total_square(l)
        inv_rep = jnp.transpose(jnp.broadcast_to(inv8[0:1], (T, T)))
        new_tokens(l, inv_rep)

        @pl.when(seg < nseg - 1)
        def _():
            remote(
                ubuf.at[l + 1, pl.ds(T - 16, 16), :], halo.at[l], hs.at[l], hr.at[l], phase, seg + 1
            ).start()

        @pl.when(l == 0)
        def _():
            weights_2(1)

        weights_2(l + 2)

        @pl.when(phase != l)
        def _():
            wait_bytes(ppb.at[l], wr.at[l, 6])

        s_u = su[l, 0] + su[l, 1] + su[l, 2] + su[l, 3]
        s_m = sm[l, 0, 0:16] + sm[l, 1, 0:16] + sm[l, 2, 0:16] + sm[l, 3, 0:16]
        pre = s_u + inv8[0:1] * s_m + ppb[l, 72:88]
        step = jnp.maximum(pre, 0.0) + jnp.log1p(jnp.exp(-jnp.abs(pre)))
        log_decay = -jnp.exp(ppb[l, 56:72]) * step
        run = jnp.dot(log_decay, sum_up, preferred_element_type=F32, precision=lax.Precision.HIGHEST)
        goes_on = sg[1, 0:1]
        is_last = sg[1, 8:9]
        cgain = jnp.exp(run) * goes_on
        tail = jnp.exp(jnp.broadcast_to(run[:, T - 1 : T], (PER, T)) - run) * is_last * step
        sg[0] = jnp.broadcast_to(cgain[:, T - 1 : T], (PER, T))
        gain8 = jnp.where(
            lane8 < 64, sg[0, pl.ds(0, 8, stride=2), :], sg[0, pl.ds(1, 8, stride=2), :]
        )
        gout[l] = gain8
        grecv[l, x] = gain8
        for d in range(1, NX):
            xd = (x + d) % NX
            remote(gout.at[l], grecv.at[l, x], xs.at[l, 1], xr.at[l, 1], phase, z * NX + xd).start()

        conv_rows(l, 16, T - 16)

        @pl.when((l == 0) & (phase > 0))
        def _():
            wait_bytes(bcu.at[0, 0], yr.at[0, 0])

        @pl.when(l > 0)
        def _():
            wait_bytes(bcu.at[l, pl.ds(0, 3)], yr.at[l, 0])
            wait_bytes(bm.at[l, pl.ds(0, 3)], yr.at[l, 2])

        def summed(ref, r0):
            r = pl.ds(r0, 64)
            return (ref[l, 0, r].astype(F32) + ref[l, 1, r].astype(F32)) + (
                ref[l, 2, r].astype(F32) + ref[l, 3, r].astype(F32)
            )

        b_cols = (summed(bcu, 0) + inv8[0:1] * summed(bm, 0)).astype(BF16)
        bt = b_cols.astype(F32)

        @pl.when(seg > 0)
        def _():
            wait_bytes(halo.at[l], hr.at[l])

        @pl.when(seg == 0)
        def _():
            halo[l] = jnp.zeros((16, CH), BF16)

        fbuf[pl.ds(0, 16), :] = halo[l].astype(F32)
        conv_rows(l, 0, 16)

        low64 = low[0:64]
        for j in range(NCH):
            cj = pl.ds(128 * j, 128)
            left = jnp.concatenate([bt * tail[2 * j : 2 * j + 1], bt * tail[2 * j + 1 : 2 * j + 2]], axis=0)
            both = jnp.dot(left.astype(BF16), inp[:, cj], preferred_element_type=F32)
            st = jnp.where(low64, both[0:64], both[64:128]).astype(BF16)
            for q in range(NX):
                lout[l, q, :, cj] = st[16 * q : 16 * q + 16]
        for d in (2, 1, 3):
            xd = (x + d) % NX
            remote(
                lout.at[l, xd], lrecv.at[l, x], xs.at[l, 0], xr.at[l, 0], phase, z * NX + xd
            ).start()
        lrecv[l, x] = lout[l, x]

        @pl.when(l > 0)
        def _():
            send_out(l)

        @pl.when(phase == l + 4)
        def _():
            send_params()
            send_weights()

        @pl.when(l > 0)
        def _():
            wait_bytes(cm.at[l, pl.ds(0, 3)], yr.at[l, 4])

        c_cols = (summed(bcu, 64) + inv8[0:1] * summed(cm, 0)).astype(BF16)
        cs = jnp.transpose(c_cols.astype(F32)).astype(BF16)
        scores = jnp.dot(cs, b_cols, preferred_element_type=F32)
        scores = scores * msk[0]
        cols = jnp.transpose(jnp.concatenate([run, cgain, jnp.zeros((T - 2 * PER, T), F32)], axis=0))
        for j in range(NCH):
            for i in range(2):
                h = 2 * j + i
                gap = jnp.broadcast_to(cols[:, h : h + 1], (T, T)) - run[h : h + 1]
                w = scores * (jnp.exp(jnp.minimum(gap, 0.0)) * step[h : h + 1])
                wts[j, :, pl.ds(128 * i, 128)] = w.astype(BF16)

        for j in range(NCH):
            cj = pl.ds(128 * j, 128)
            v = inp[:, cj]
            vf = v.astype(F32)
            right = jnp.concatenate([jnp.where(low, vf, 0.0), jnp.where(low, 0.0, vf)], axis=0).astype(BF16)
            intra = jnp.dot(wts[j], right, preferred_element_type=F32)
            m0[:, cj] = intra + ppb[l, pl.ds(48 + j, 1), :] * vf

        wait_bytes(grecv.at[l, pl.ds(0, 3)], xr.at[l, 1])
        wait_bytes(lrecv.at[l, pl.ds(0, 3)], xr.at[l, 0])
        p1 = grecv[l, 0]
        p2 = p1 * grecv[l, 1]
        p3 = p2 * grecv[l, 2]
        ggout[l] = p3 * grecv[l, 3]
        ga = grecv[l, 1]
        gb = grecv[l, 2]
        gc = grecv[l, 3]
        for j in range(NCH):
            cj = pl.ds(128 * j, 128)
            r1 = lrecv[l, 0, :, cj].astype(F32)
            r2 = lrecv[l, 1, :, cj].astype(F32) + ga[j : j + 1] * r1
            r3 = lrecv[l, 2, :, cj].astype(F32) + gb[j : j + 1] * r2
            rt = lrecv[l, 3, :, cj].astype(F32) + gc[j : j + 1] * r3
            rb[0, :, cj] = r1
            rb[1, :, cj] = r2
            rb[2, :, cj] = r3
            tout[l, :, cj] = rt.astype(BF16)
        for d in range(1, REACH + 1):

            @pl.when(z + d < nz)
            def _(d=d):
                to = (z + d) * NX + x
                remote(
                    ggout.at[l], ggrecv.at[l, d - 1], zs.at[l, REACH + d - 1], zr.at[l, REACH + d - 1], phase, to
                ).start()
                remote(tout.at[l], trecv.at[l, d - 1], zs.at[l, d - 1], zr.at[l, d - 1], phase, to).start()

        n = l + 1

        @pl.when(n < LAYERS)
        def _():
            @pl.when(l == 0)
            def _():
                weights_3(n)

            weights_4(n)
            a = product(wbuf[l], ubuf[l + 1])
            for g in range(GROUPS):
                bcuo[n, g] = rows_of(a, g)
                suo[n, g] = a[512 + 16 * g : 528 + 16 * g]
            push(n, 1, suo, su)
            push(n, 0, bcuo, bcu)

        for d in range(1, REACH + 1):

            @pl.when(z >= d)
            def _(d=d):
                wait_bytes(ggrecv.at[l, d - 1], zr.at[l, REACH + d - 1])
                wait_bytes(trecv.at[l, d - 1], zr.at[l, d - 1])

            @pl.when(z < d)
            def _(d=d):
                ggrecv[l, d - 1] = jnp.zeros((8, 128), F32)
                trecv[l, d - 1] = jnp.zeros((16, CH), BF16)

        for j in range(NCH):
            cj = pl.ds(128 * j, 128)
            e = trecv[l, 3, :, cj].astype(F32)
            for d in (2, 1, 0):
                e = trecv[l, d, :, cj].astype(F32) + ggrecv[l, d, pl.ds(j, 1), :] * e
            eout[l, 0, :, cj] = e.astype(BF16)
            eout[l, 1, :, cj] = (rb[0, :, cj] + p1[j : j + 1] * e).astype(BF16)
            eout[l, 2, :, cj] = (rb[1, :, cj] + p2[j : j + 1] * e).astype(BF16)
            eout[l, 3, :, cj] = (rb[2, :, cj] + p3[j : j + 1] * e).astype(BF16)
        for d in (2, 1, 3):
            xd = (x + d) % NX
            remote(
                eout.at[l, xd], ent.at[l, x], xs.at[l, 2], xr.at[l, 2], phase, z * NX + xd
            ).start()
        ent[l, x] = eout[l, x]

        for j in range(NCH):
            g0 = jnp.broadcast_to(cols[:, PER + 2 * j : PER + 2 * j + 1], (T, T))
            g1 = jnp.broadcast_to(cols[:, PER + 2 * j + 1 : PER + 2 * j + 2], (T, T))
            gx[:, pl.ds(128 * j, 128)] = jnp.where(low, g0, g1)
        wait_bytes(ent.at[l, pl.ds(0, 3)], xr.at[l, 2])
        weights_1(n + 2)
        sq = jnp.zeros((T, 128), F32)
        for j in range(NCH):
            cj = pl.ds(128 * j, 128)
            part = jnp.dot(cs, ent[l, :, :, cj].reshape(STATE, 128), preferred_element_type=F32)
            mixed = m0[:, cj] + part * gx[:, cj]
            sq = sq + mixed * mixed
            scaled = ppb[l, pl.ds(40 + j, 1), :] * mixed
            gm[:, cj] = scaled
            gmb[:, cj] = scaled.astype(BF16)
        sq_row = jnp.broadcast_to(jnp.sum(jnp.transpose(sq), axis=0, keepdims=True), (8, T))
        for g in range(GROUPS):
            smo[n, g, 16:24] = sq_row

        @pl.when(n < LAYERS)
        def _():
            v = gmb[...]
            a = product(wbuf[l, 512:576, :], v)
            for g in range(GROUPS):
                smo[n, g, 0:16] = a[16 * g : 16 * g + 16]
            push(n, 3, smo, sm)
            a = product(wbuf[l, 0:256, :], v).astype(BF16)
            for g in range(GROUPS):
                bmo[n, g] = a[64 * g : 64 * g + 64]
            push(n, 2, bmo, bm)
            a = product(wbuf[l, 256:512, :], v).astype(BF16)
            for g in range(GROUPS):
                cmo[n, g] = a[64 * g : 64 * g + 64]
            push(n, 4, cmo, cm)

        @pl.when(n == LAYERS)
        def _():
            for g in range(GROUPS):
                smo[n, g, 0:16] = jnp.zeros((16, 128), F32)
            push(n, 3, smo, sm)

        weights_3(n + 1)
        return carry

    lax.fori_loop(0, LAYERS, layer, 0)

    wait_square(LAYERS)
    inv8 = total_square(LAYERS)
    new_tokens(LAYERS, jnp.transpose(jnp.broadcast_to(inv8[0:1], (T, T))))
    send_out(LAYERS)

    def drain(l, carry):
        n = l + 1

        @pl.when(n < LAYERS)
        def _():
            wait_bytes(bcuo.at[n, pl.ds(0, 3)], ys.at[n, 0])
            wait_bytes(suo.at[n, pl.ds(0, 3)], ys.at[n, 1])
            wait_bytes(bmo.at[n, pl.ds(0, 3)], ys.at[n, 2])
            wait_bytes(cmo.at[n, pl.ds(0, 3)], ys.at[n, 4])

        wait_bytes(smo.at[n, pl.ds(0, 3)], ys.at[n, 3])
        wait_bytes(ubuf.at[n + 1], outs.at[n])
        wait_bytes(lout.at[l, pl.ds(0, 3)], xs.at[l, 0])
        wait_bytes(grecv.at[l, pl.ds(0, 3)], xs.at[l, 1])
        wait_bytes(eout.at[l, pl.ds(0, 3)], xs.at[l, 2])
        for d in range(1, REACH + 1):

            @pl.when(z + d < nz)
            def _(d=d):
                wait_bytes(ggout.at[l], zs.at[l, REACH + d - 1])
                wait_bytes(tout.at[l], zs.at[l, d - 1])

        @pl.when(seg < nseg - 1)
        def _():
            wait_bytes(halo.at[l], hs.at[l])

        @pl.when(relays(n))
        def _():
            wait_bytes(wbuf.at[l], wrs.at[n])
            for i, rows in enumerate((WPART, WPART, WHALF, WPART - WHALF)):
                wait_bytes(part(n, x, 0, rows), wxs.at[n, i])

        @pl.when(phase != l)
        def _():
            wait_bytes(ubuf.at[0], outr.at[l])
            wait_bytes(ppb.at[l], ppsem.at[l])

        return carry

    lax.fori_loop(0, LAYERS, drain, 0)

    @pl.when(phase > 0)
    def _():
        for dy in range(1, NY):
            wait_bytes(part(1, x, 0, WPART), wss.at[(y + dy) % NY])
        wait_bytes(wbuf.at[0], wss.at[y])

    @pl.when(phase == 0)
    def _():
        for p in range(1, NY * NC):
            wait_bytes(bcuo.at[0, 0], p0s.at[p, 0])
            wait_bytes(suo.at[0, 0], p0s.at[p, 1])

    @pl.when(seg < nseg - 1)
    def _():
        wait_bytes(idsrc, idsem.at[0])


def body(
    stream, doc_ids, in_proj, conv_weight, conv_bias, decay_log, step_bias, skip_gain, norm_gain
):
    nseg = lax.axis_size("seg")
    nz = nseg // NX

    vmem = pltpu.VMEM
    dma = pltpu.SemaphoreType.DMA
    n1 = LAYERS + 1
    return pl.pallas_call(
        functools.partial(kernel, nz),
        out_shape=jax.ShapeDtypeStruct((1, MICRO, T, CH * GROUPS), BF16),
        in_specs=[
            pl.BlockSpec(memory_space=pl.ANY),
            pl.BlockSpec(memory_space=pltpu.VMEM),
            pl.BlockSpec(memory_space=pl.ANY),
        ]
        + [pl.BlockSpec(memory_space=pltpu.VMEM)] * 6,
        out_specs=pl.BlockSpec(memory_space=pl.ANY),
        scratch_shapes=[
            vmem((LAYERS - 1, PROJ, CH), BF16),
            vmem((PROJ, CH * GROUPS), BF16),
            vmem((MICRO, T, CH * GROUPS), BF16),
            vmem((LAYERS + 2, T, CH), BF16),
            vmem((T, CH), F32),
            vmem((T, CH), BF16),
            vmem((GROUPS, 88, 128), F32),
            vmem((HEADS, 128), F32),
            vmem((PROJ, T), F32),
            vmem((LAYERS, 88, 128), F32),
            vmem((8, T), jnp.int32),
            vmem((8, T), jnp.int32),
            vmem((KERNEL, T, T), F32),
            vmem((LAYERS, 16, CH), BF16),
            vmem((T + 16, CH), F32),
            vmem((T, CH), BF16),
            vmem((NCH, T, 256), BF16),
            vmem((n1, NY, T, 128), BF16),
            vmem((n1, NY, 64, 128), BF16),
            vmem((n1, NY, 64, 128), BF16),
            vmem((n1, NY, T, 128), BF16),
            vmem((n1, NY, 64, 128), BF16),
            vmem((n1, NY, 64, 128), BF16),
            vmem((n1, NY, 16, 128), F32),
            vmem((n1, NY, 24, 128), F32),
            vmem((n1, NY, 16, 128), F32),
            vmem((n1, NY, 24, 128), F32),
            vmem((2, 16, 128), F32),
            vmem((LAYERS, NX, 16, CH), BF16),
            vmem((LAYERS, NX, 16, CH), BF16),
            vmem((LAYERS, 8, 128), F32),
            vmem((LAYERS, NX, 8, 128), F32),
            vmem((LAYERS, 16, CH), BF16),
            vmem((LAYERS, 8, 128), F32),
            vmem((LAYERS, REACH, 16, CH), BF16),
            vmem((LAYERS, REACH, 8, 128), F32),
            vmem((3, 16, CH), F32),
            vmem((LAYERS, NX, 16, CH), BF16),
            vmem((LAYERS, NX, 16, CH), BF16),
            vmem((T, CH), F32),
            vmem((T, CH), F32),
            dma((n1, 5)),
            dma((n1, 5)),
            dma((NY * NC, 2)),
            dma((LAYERS, 3)),
            dma((LAYERS, 3)),
            dma((LAYERS, 2 * REACH)),
            dma((LAYERS, 2 * REACH)),
            dma((LAYERS,)),
            dma((LAYERS,)),
            dma((LAYERS, 7)),
            dma((NY,)),
            dma((LAYERS,)),
            dma((LAYERS, 4)),
            dma((NY * NC,)),
            dma((NY * NC,)),
            dma((n1,)),
            dma((2,)),
            dma((4,)),
        ],
        compiler_params=pltpu.CompilerParams(
            collective_id=0, has_side_effects=True, vmem_limit_bytes=60 * 1024 * 1024
        ),
    )(
        stream,
        doc_ids,
        jnp.swapaxes(in_proj, 1, 2),
        conv_weight,
        conv_bias,
        decay_log,
        step_bias,
        skip_gain,
        norm_gain,
    )


def solution(mesh):
    placed = (
        P(None, "seg", None),
        P(None, "seg"),
        P("phase", None, None),
        P("phase", None, None),
        P("phase", None),
        P("phase", None),
        P("phase", None),
        P("phase", None),
        P("phase", None),
    )
    return jax.shard_map(
        body, mesh=mesh, in_specs=placed, out_specs=P("phase", None, "seg", None), check_vma=False
    )
```

```python
import functools

import jax
import jax.numpy as jnp
from jax import lax
from jax.experimental import pallas as pl
from jax.experimental.pallas import tpu as pltpu
from jax.sharding import PartitionSpec as P

NY = 4
NC = 2
NX = 4
LAYERS = 8
HEADS = 64
HEAD_DIM = 64
STATE = 64
GROUPS = 4
KERNEL = 4
MICRO = 2
T = 128
CH = 1024
PER = 16
NCH = 8
REACH = 4
PROJ = 576
WPART = 144
WHALF = 80
MESH = pl.DeviceIdType.MESH
F32 = jnp.float32
BF16 = jnp.bfloat16


def wait_bytes(ref, sem):
    pltpu.make_async_copy(ref, ref, sem).wait()


def kernel(
    nz,
    stream_ref,
    ids_ref,
    proj_ref,
    convw_ref,
    convb_ref,
    decay_ref,
    stepb_ref,
    skip_ref,
    norm_ref,
    out_ref,
    wbuf,
    w0,
    strm,
    ubuf,
    gm,
    gmb,
    pps,
    pph,
    p0,
    ppb,
    idsrc,
    idh,
    msk,
    halo,
    fbuf,
    inp,
    wts,
    bcu,
    bm,
    cm,
    bcuo,
    bmo,
    cmo,
    su,
    sm,
    suo,
    smo,
    sg,
    lout,
    lrecv,
    gout,
    grecv,
    tout,
    ggout,
    trecv,
    ggrecv,
    rb,
    eout,
    ent,
    m0,
    gx,
    yr,
    ys,
    p0s,
    xr,
    xs,
    zr,
    zs,
    hr,
    hs,
    wr,
    wss,
    wrs,
    wxs,
    ppsem,
    outr,
    outs,
    idsem,
    loc,
):
    phase = lax.axis_index("phase")
    seg = lax.axis_index("seg")
    nseg = nz * NX
    y = phase // NC
    c = phase % NC
    z = seg // NX
    x = seg % NX

    def remote(src, dst, ssem, rsem, p, s):
        return pltpu.make_async_remote_copy(
            src_ref=src,
            dst_ref=dst,
            send_sem=ssem,
            recv_sem=rsem,
            device_id=(p, s),
            device_id_type=MESH,
        )

    barrier = pltpu.get_barrier_semaphore()
    count = 0
    for d in range(1, NY * NC):
        pl.semaphore_signal(barrier, inc=1, device_id=((phase + d) % (NY * NC), seg), device_id_type=MESH)
        count += 1
    for d in range(1, NX):
        pl.semaphore_signal(
            barrier, inc=1, device_id=(phase, z * NX + (x + d) % NX), device_id_type=MESH
        )
        count += 1
    for d in range(1, nz):
        pl.semaphore_signal(
            barrier, inc=1, device_id=(phase, ((z + d) % nz) * NX + x), device_id_type=MESH
        )
        count += 1
    for d in (1, nseg - 1):
        pl.semaphore_signal(barrier, inc=1, device_id=(phase, (seg + d) % nseg), device_id_type=MESH)
        count += 1

    cp_u = pltpu.make_async_copy(
        stream_ref.at[c, :, pl.ds(pl.multiple_of(y * CH, CH), CH)], ubuf.at[0], loc.at[0]
    )
    cp_u.start()
    def quarter(g):
        return proj_ref.at[0, :, pl.ds(pl.multiple_of(g * CH, CH), CH)]

    cp_w0 = pltpu.make_async_copy(proj_ref.at[0], w0, loc.at[1])
    cp_s0 = pltpu.make_async_copy(stream_ref, strm, loc.at[3])

    @pl.when(phase == 0)
    def _():
        cp_w0.start()
        cp_s0.start()

    @pl.when(phase > 0)
    def _():
        pltpu.make_async_copy(quarter(y), wbuf.at[phase - 1], loc.at[2]).start()

    low8 = lax.broadcasted_iota(jnp.int32, (8, 128), 1) < 64
    for g in range(GROUPS):
        for j in range(NCH):
            cj = pl.ds(CH * g + 128 * j, 128)
            for k in range(KERNEL):
                pps[g, pl.ds(8 * k + j, 1), :] = convw_ref[0, pl.ds(k, 1), cj]
            pps[g, pl.ds(32 + j, 1), :] = convb_ref[:, cj]
            pps[g, pl.ds(40 + j, 1), :] = norm_ref[:, cj]

    def per_head(ref):
        return jnp.transpose(jnp.broadcast_to(ref[...], (128, HEADS)))

    pph[...] = per_head(skip_ref)
    decay_rows = per_head(decay_ref)
    stepb_rows = per_head(stepb_ref)
    for g in range(GROUPS):
        pps[g, 48:56] = jnp.where(
            low8, pph[pl.ds(PER * g, 8, stride=2), :], pph[pl.ds(PER * g + 1, 8, stride=2), :]
        )
        pps[g, 56:72] = decay_rows[PER * g : PER * g + PER]
        pps[g, 72:88] = stepb_rows[PER * g : PER * g + PER]
    ppb[phase] = pps[y]

    pl.semaphore_wait(barrier, count)

    idsrc[...] = jnp.broadcast_to(ids_ref[pl.ds(c, 1), :], (8, T))

    @pl.when(seg < nseg - 1)
    def _():
        remote(idsrc, idh, idsem.at[0], idsem.at[1], phase, seg + 1).start()

    @pl.when(seg == 0)
    def _():
        idh[...] = jnp.full((8, T), -1, jnp.int32)

    def send_params():
        for d in range(1, NY * NC):
            p = (phase + d) % (NY * NC)
            remote(pps.at[p // NC], ppb.at[phase], ppsem.at[p], wr.at[phase, 6], p, seg).start()

    def piece(n, i, r0, rows):
        return wbuf.at[n - 1, pl.ds(pl.multiple_of(i * WPART + r0, 16), rows), :]

    def send_weights():
        rows = pl.ds(pl.multiple_of(x * WPART, 16), WPART)
        for dy in (2, 1, 3):
            yd = (y + dy) % NY
            remote(
                proj_ref.at[0, rows, pl.ds(pl.multiple_of(yd * CH, CH), CH)],
                piece(phase, x, 0, WPART),
                wss.at[yd],
                wr.at[phase, 0],
                yd * NC + c,
                seg,
            ).start()
        remote(quarter(y), wbuf.at[phase - 1], wss.at[y], wr.at[phase, 5], y * NC + 1 - c, seg).start()

    def relays(n):
        return (n < LAYERS) & (c == n % NC) & (y != n // NC)

    right = z * NX + (x + 1) % NX
    left = z * NX + (x + NX - 1) % NX

    def weights_1(n):
        @pl.when(relays(n))
        def _():
            mine = piece(n, x, 0, WPART)
            wait_bytes(mine, wr.at[n, 0])
            remote(mine, mine, wxs.at[n, 0], wr.at[n, 1], phase, right).start()
            remote(mine, mine, wxs.at[n, 1], wr.at[n, 2], phase, left).start()

    def weights_2(n):
        @pl.when(relays(n))
        def _():
            wait_bytes(piece(n, x, 0, WPART), wr.at[n, 1])
            first = piece(n, (x + NX - 1) % NX, 0, WHALF)
            remote(first, first, wxs.at[n, 2], wr.at[n, 3], phase, right).start()
            wait_bytes(piece(n, x, 0, WPART), wr.at[n, 2])
            last = piece(n, (x + 1) % NX, WHALF, WPART - WHALF)
            remote(last, last, wxs.at[n, 3], wr.at[n, 4], phase, left).start()

    def weights_3(n):
        @pl.when(relays(n))
        def _():
            wait_bytes(piece(n, x, 0, WHALF), wr.at[n, 3])
            wait_bytes(piece(n, x, 0, WPART - WHALF), wr.at[n, 4])
            whole = wbuf.at[n - 1]
            remote(whole, whole, wrs.at[n], wr.at[n, 5], y * NC + 1 - c, seg).start()

    def weights_4(n):
        @pl.when((n < LAYERS) & (c != n % NC))
        def _():
            wait_bytes(wbuf.at[n - 1], wr.at[n, 5])

    lane = lax.broadcasted_iota(jnp.int32, (T, 128), 1)
    low = lane < 64

    def product(w, a):
        return lax.dot_general(w, a, (((1,), (1,)), ((), ())), preferred_element_type=F32)

    def rows_of(a, g):
        return jnp.concatenate(
            [a[64 * g : 64 * g + 64], a[256 + 64 * g : 320 + 64 * g]], axis=0
        ).astype(BF16)

    @pl.when(phase == 0)
    def _():
        send_params()
        cp_w0.wait()
        cp_s0.wait()
        for m in range(MICRO):
            at = LAYERS * m
            mine = strm[m]
            for r in range(4):
                rr = pl.ds(WPART * r, WPART)
                p0[rr, :] = product(w0[rr, :], mine)
            for g in range(GROUPS):
                bcuo[at, g, 0:64] = p0[pl.ds(64 * g, 64), :].astype(BF16)
                bcuo[at, g, 64:128] = p0[pl.ds(256 + 64 * g, 64), :].astype(BF16)
                suo[at, g] = p0[pl.ds(512 + 16 * g, 16), :]
            for g in (2, 1, 3, 0):
                p = g * NC + m
                if p > 0:
                    remote(bcuo.at[at, g], bcu.at[0, 0], p0s.at[p, 0], yr.at[0, 0], p, seg).start()
                    remote(suo.at[at, g], su.at[0, 0], p0s.at[p, 1], yr.at[0, 1], p, seg).start()
        bcu[0, 0] = bcuo[0, 0]
        su[0, 0] = suo[0, 0]

    @pl.when((phase >= 1) & (phase <= 3))
    def _():
        send_params()
        send_weights()

    cp_u.wait()

    @pl.when(phase > 0)
    def _():
        pltpu.make_async_copy(quarter(y), wbuf.at[phase - 1], loc.at[2]).wait()

    bm[0] = jnp.zeros((NY, 64, 128), BF16)
    cm[0] = jnp.zeros((NY, 64, 128), BF16)
    sm[0] = jnp.zeros((NY, 24, 128), F32)
    for s in range(1, NY):
        bcu[0, s] = jnp.zeros((T, 128), BF16)
        su[0, s] = jnp.zeros((16, 128), F32)
    gm[...] = jnp.zeros((T, CH), F32)

    @pl.when(seg > 0)
    def _():
        wait_bytes(idh, idsem.at[1])

    own_row = idsrc[...].astype(F32)
    prior_row = idh[...].astype(F32)
    lane8 = lax.broadcasted_iota(jnp.int32, (8, T), 1)
    row_rep = jnp.broadcast_to(own_row[0:1], (T, T))
    col_rep = jnp.transpose(row_rep)
    t_at = lax.broadcasted_iota(jnp.int32, (T, T), 0)
    msk[0] = jnp.where((row_rep == col_rep) & (t_at >= lane), 1.0, 0.0)
    for k in range(1, KERNEL):
        behind = jnp.where(lane8 < k, pltpu.roll(prior_row, k, 1), pltpu.roll(own_row, k, 1))
        same = jnp.where(behind == own_row, 1.0, 0.0)
        msk[k] = jnp.transpose(jnp.broadcast_to(same[0:1], (T, T)))
    prior_last = jnp.broadcast_to(prior_row[:, T - 1 : T], (8, T))
    own_last = jnp.broadcast_to(own_row[:, T - 1 : T], (8, T))
    sg[1, 0:8] = jnp.where(own_row == prior_last, 1.0, 0.0)
    sg[1, 8:16] = jnp.where(own_row == own_last, 1.0, 0.0)
    sum_up = jnp.where(t_at <= lane, 1.0, 0.0)
    weights_1(1)

    def total_square(lx):
        s = sm[lx, 0, 16:24] + sm[lx, 1, 16:24] + sm[lx, 2, 16:24] + sm[lx, 3, 16:24]
        return lax.rsqrt(s * (1.0 / (CH * GROUPS)) + 1e-05)

    def new_tokens(lx, inv_rep):
        for j in range(NCH):
            cj = pl.ds(128 * j, 128)
            u = ubuf[lx, :, cj].astype(F32) + gm[:, cj] * inv_rep
            ub = u.astype(BF16)
            ubuf[lx + 1, :, cj] = ub
            fbuf[pl.ds(16, T), cj] = ub.astype(F32)

    def send_out(lx):
        there = out_ref.at[0, c, :, pl.ds(pl.multiple_of(y * CH, CH), CH)]

        @pl.when(phase == lx - 1)
        def _():
            pltpu.make_async_copy(ubuf.at[lx + 1], there, outs.at[lx]).start()

        @pl.when(phase != lx - 1)
        def _():
            remote(ubuf.at[lx + 1], there, outs.at[lx], outr.at[phase], lx - 1, seg).start()

    def wait_square(lx):
        wait_bytes(sm.at[lx, pl.ds(0, 3)], yr.at[lx, 3])

    def push(lx, kind, outbuf, inbuf):
        for dy in (2, 1, 3):
            yd = (y + dy) % NY
            remote(
                outbuf.at[lx, yd], inbuf.at[lx, y], ys.at[lx, kind], yr.at[lx, kind], yd * NC + c, seg
            ).start()
        inbuf[lx, y] = outbuf[lx, y]

    def conv_rows(l, r0, n):
        for j in range(NCH):
            cj = pl.ds(128 * j, 128)
            acc = fbuf[pl.ds(16 + r0, n), cj] * ppb[l, pl.ds(24 + j, 1), :] + ppb[l, pl.ds(32 + j, 1), :]
            for k in range(1, KERNEL):
                tap = ppb[l, pl.ds(8 * (3 - k) + j, 1), :]
                acc = acc + (fbuf[pl.ds(16 + r0 - k, n), cj] * msk[k, pl.ds(r0, n), :]) * tap
            inp[pl.ds(r0, n), cj] = (acc * (1.0 / (1.0 + jnp.exp(-acc)))).astype(BF16)

    def layer(l, carry):
        @pl.when((l == 0) & (phase > 0))
        def _():
            wait_bytes(su.at[0, 0], yr.at[0, 1])

        @pl.when(l > 0)
        def _():
            wait_bytes(su.at[l, pl.ds(0, 3)], yr.at[l, 1])
            wait_square(l)

        inv8 = total_square(l)
        inv_rep = jnp.transpose(jnp.broadcast_to(inv8[0:1], (T, T)))
        new_tokens(l, inv_rep)

        @pl.when(seg < nseg - 1)
        def _():
            remote(
                ubuf.at[l + 1, pl.ds(T - 16, 16), :], halo.at[l], hs.at[l], hr.at[l], phase, seg + 1
            ).start()

        @pl.when(l > 0)
        def _():
            weights_3(l + 1)

        @pl.when(phase != l)
        def _():
            wait_bytes(ppb.at[l], wr.at[l, 6])

        s_u = su[l, 0] + su[l, 1] + su[l, 2] + su[l, 3]
        s_m = sm[l, 0, 0:16] + sm[l, 1, 0:16] + sm[l, 2, 0:16] + sm[l, 3, 0:16]
        pre = s_u + inv8[0:1] * s_m + ppb[l, 72:88]
        step = jnp.maximum(pre, 0.0) + jnp.log1p(jnp.exp(-jnp.abs(pre)))
        log_decay = -jnp.exp(ppb[l, 56:72]) * step
        run = jnp.dot(log_decay, sum_up, preferred_element_type=F32, precision=lax.Precision.HIGHEST)
        goes_on = sg[1, 0:1]
        is_last = sg[1, 8:9]
        cgain = jnp.exp(run) * goes_on
        tail = jnp.exp(jnp.broadcast_to(run[:, T - 1 : T], (PER, T)) - run) * is_last * step
        sg[0] = jnp.broadcast_to(cgain[:, T - 1 : T], (PER, T))
        gain8 = jnp.where(
            lane8 < 64, sg[0, pl.ds(0, 8, stride=2), :], sg[0, pl.ds(1, 8, stride=2), :]
        )
        gout[l] = gain8
        grecv[l, x] = gain8
        for d in range(1, NX):
            xd = (x + d) % NX
            remote(gout.at[l], grecv.at[l, x], xs.at[l, 4], xr.at[l, 4], phase, z * NX + xd).start()

        conv_rows(l, 16, T - 16)

        @pl.when((l == 0) & (phase > 0))
        def _():
            wait_bytes(bcu.at[0, 0], yr.at[0, 0])

        @pl.when(l > 0)
        def _():
            wait_bytes(bcu.at[l, pl.ds(0, 3)], yr.at[l, 0])
            wait_bytes(bm.at[l, pl.ds(0, 3)], yr.at[l, 2])

        def summed(ref, r0):
            r = pl.ds(r0, 64)
            return (ref[l, 0, r].astype(F32) + ref[l, 1, r].astype(F32)) + (
                ref[l, 2, r].astype(F32) + ref[l, 3, r].astype(F32)
            )

        b_cols = (summed(bcu, 0) + inv8[0:1] * summed(bm, 0)).astype(BF16)
        bt = b_cols.astype(F32)

        @pl.when(seg > 0)
        def _():
            wait_bytes(halo.at[l], hr.at[l])

        @pl.when(seg == 0)
        def _():
            halo[l] = jnp.zeros((16, CH), BF16)

        fbuf[pl.ds(0, 16), :] = halo[l].astype(F32)
        conv_rows(l, 0, 16)

        low64 = low[0:64]
        for half in range(2):
            for j in range(4 * half, 4 * half + 4):
                ch = pl.ds(128 * (j % 4), 128)
                left = jnp.concatenate([bt * tail[2 * j : 2 * j + 1], bt * tail[2 * j + 1 : 2 * j + 2]], axis=0)
                both = jnp.dot(left.astype(BF16), inp[:, pl.ds(128 * j, 128)], preferred_element_type=F32)
                st = jnp.where(low64, both[0:64], both[64:128]).astype(BF16)
                for q in range(NX):
                    lout[l, half, q, :, ch] = st[16 * q : 16 * q + 16]
            for d in (2, 1, 3):
                xd = (x + d) % NX
                remote(
                    lout.at[l, half, xd],
                    lrecv.at[l, half, x],
                    xs.at[l, half],
                    xr.at[l, half],
                    phase,
                    z * NX + xd,
                ).start()
            lrecv[l, half, x] = lout[l, half, x]

        @pl.when(l > 0)
        def _():
            send_out(l)

        @pl.when(phase == l + 4)
        def _():
            send_params()
            send_weights()

        @pl.when(l == 0)
        def _():
            weights_2(1)
            weights_1(2)

        @pl.when(l > 0)
        def _():
            wait_bytes(cm.at[l, pl.ds(0, 3)], yr.at[l, 4])

        c_cols = (summed(bcu, 64) + inv8[0:1] * summed(cm, 0)).astype(BF16)
        cs = jnp.transpose(c_cols.astype(F32)).astype(BF16)
        scores = jnp.dot(cs, b_cols, preferred_element_type=F32)
        scores = scores * msk[0]
        cols = jnp.transpose(jnp.concatenate([run, cgain, jnp.zeros((T - 2 * PER, T), F32)], axis=0))
        for j in range(NCH):
            for i in range(2):
                h = 2 * j + i
                gap = jnp.broadcast_to(cols[:, h : h + 1], (T, T)) - run[h : h + 1]
                w = scores * (jnp.exp(jnp.minimum(gap, 0.0)) * step[h : h + 1])
                wts[j, :, pl.ds(128 * i, 128)] = w.astype(BF16)

        for j in range(NCH):
            cj = pl.ds(128 * j, 128)
            v = inp[:, cj]
            vf = v.astype(F32)
            right = jnp.concatenate([jnp.where(low, vf, 0.0), jnp.where(low, 0.0, vf)], axis=0).astype(BF16)
            intra = jnp.dot(wts[j], right, preferred_element_type=F32)
            m0[:, cj] = intra + ppb[l, pl.ds(48 + j, 1), :] * vf

        wait_bytes(grecv.at[l, pl.ds(0, 3)], xr.at[l, 4])
        p1 = grecv[l, 0]
        p2 = p1 * grecv[l, 1]
        p3 = p2 * grecv[l, 2]
        ggout[l] = p3 * grecv[l, 3]
        ga = grecv[l, 1]
        gb = grecv[l, 2]
        gc = grecv[l, 3]
        n = l + 1
        for half in range(2):
            wait_bytes(lrecv.at[l, half, pl.ds(0, 3)], xr.at[l, half])
            for j in range(4 * half, 4 * half + 4):
                cj = pl.ds(128 * j, 128)
                ch = pl.ds(128 * (j % 4), 128)
                r1 = lrecv[l, half, 0, :, ch].astype(F32)
                r2 = lrecv[l, half, 1, :, ch].astype(F32) + ga[j : j + 1] * r1
                r3 = lrecv[l, half, 2, :, ch].astype(F32) + gb[j : j + 1] * r2
                rt = lrecv[l, half, 3, :, ch].astype(F32) + gc[j : j + 1] * r3
                rb[0, :, cj] = r1
                rb[1, :, cj] = r2
                rb[2, :, cj] = r3
                tout[l, half, :, ch] = rt.astype(BF16)
            for d in range(1, REACH + 1):

                @pl.when(z + d < nz)
                def _(d=d, half=half):
                    to = (z + d) * NX + x
                    if half == 0:
                        remote(
                            ggout.at[l], ggrecv.at[l, d - 1], zs.at[l, 2, d - 1], zr.at[l, 2, d - 1], phase, to
                        ).start()
                    remote(
                        tout.at[l, half],
                        trecv.at[l, half, d - 1],
                        zs.at[l, half, d - 1],
                        zr.at[l, half, d - 1],
                        phase,
                        to,
                    ).start()

            for d in range(1, REACH + 1):

                @pl.when(z >= d)
                def _(d=d, half=half):
                    if half == 0:
                        wait_bytes(ggrecv.at[l, d - 1], zr.at[l, 2, d - 1])
                    wait_bytes(trecv.at[l, half, d - 1], zr.at[l, half, d - 1])

                @pl.when(z < d)
                def _(d=d, half=half):
                    if half == 0:
                        ggrecv[l, d - 1] = jnp.zeros((8, 128), F32)
                    trecv[l, half, d - 1] = jnp.zeros((16, CH // 2), BF16)

            for j in range(4 * half, 4 * half + 4):
                cj = pl.ds(128 * j, 128)
                ch = pl.ds(128 * (j % 4), 128)
                e = trecv[l, half, 3, :, ch].astype(F32)
                for d in (2, 1, 0):
                    e = trecv[l, half, d, :, ch].astype(F32) + ggrecv[l, d, pl.ds(j, 1), :] * e
                eout[l, half, 0, :, ch] = e.astype(BF16)
                eout[l, half, 1, :, ch] = (rb[0, :, cj] + p1[j : j + 1] * e).astype(BF16)
                eout[l, half, 2, :, ch] = (rb[1, :, cj] + p2[j : j + 1] * e).astype(BF16)
                eout[l, half, 3, :, ch] = (rb[2, :, cj] + p3[j : j + 1] * e).astype(BF16)
            for d in (2, 1, 3):
                xd = (x + d) % NX
                remote(
                    eout.at[l, half, xd],
                    ent.at[l, half, x],
                    xs.at[l, 2 + half],
                    xr.at[l, 2 + half],
                    phase,
                    z * NX + xd,
                ).start()
            ent[l, half, x] = eout[l, half, x]


        @pl.when(n < LAYERS)
        def _():
            @pl.when(l == 0)
            def _():
                weights_3(n)

            weights_4(n)
            a = product(wbuf[l], ubuf[l + 1])
            for g in range(GROUPS):
                bcuo[n, g] = rows_of(a, g)
                suo[n, g] = a[512 + 16 * g : 528 + 16 * g]
            push(n, 1, suo, su)
            push(n, 0, bcuo, bcu)

        for j in range(NCH):
            g0 = jnp.broadcast_to(cols[:, PER + 2 * j : PER + 2 * j + 1], (T, T))
            g1 = jnp.broadcast_to(cols[:, PER + 2 * j + 1 : PER + 2 * j + 2], (T, T))
            gx[:, pl.ds(128 * j, 128)] = jnp.where(low, g0, g1)
        sq = jnp.zeros((T, 128), F32)
        for half in range(2):
            wait_bytes(ent.at[l, half, pl.ds(0, 3)], xr.at[l, 2 + half])
            if half == 1:
                weights_2(n + 1)
                weights_1(n + 2)
            for j in range(4 * half, 4 * half + 4):
                cj = pl.ds(128 * j, 128)
                state = ent[l, half, :, :, pl.ds(128 * (j % 4), 128)].reshape(STATE, 128)
                part = jnp.dot(cs, state, preferred_element_type=F32)
                mixed = m0[:, cj] + part * gx[:, cj]
                sq = sq + mixed * mixed
                scaled = ppb[l, pl.ds(40 + j, 1), :] * mixed
                gm[:, cj] = scaled
                gmb[:, cj] = scaled.astype(BF16)
        sq_row = jnp.broadcast_to(jnp.sum(jnp.transpose(sq), axis=0, keepdims=True), (8, T))
        for g in range(GROUPS):
            smo[n, g, 16:24] = sq_row

        @pl.when(n < LAYERS)
        def _():
            v = gmb[...]
            a = product(wbuf[l, 512:576, :], v)
            for g in range(GROUPS):
                smo[n, g, 0:16] = a[16 * g : 16 * g + 16]
            push(n, 3, smo, sm)
            a = product(wbuf[l, 0:256, :], v).astype(BF16)
            for g in range(GROUPS):
                bmo[n, g] = a[64 * g : 64 * g + 64]
            push(n, 2, bmo, bm)
            a = product(wbuf[l, 256:512, :], v).astype(BF16)
            for g in range(GROUPS):
                cmo[n, g] = a[64 * g : 64 * g + 64]
            push(n, 4, cmo, cm)

        @pl.when(n == LAYERS)
        def _():
            for g in range(GROUPS):
                smo[n, g, 0:16] = jnp.zeros((16, 128), F32)
            push(n, 3, smo, sm)

        return carry

    lax.fori_loop(0, LAYERS, layer, 0)

    wait_square(LAYERS)
    inv8 = total_square(LAYERS)
    new_tokens(LAYERS, jnp.transpose(jnp.broadcast_to(inv8[0:1], (T, T))))
    send_out(LAYERS)

    def drain(l, carry):
        n = l + 1

        @pl.when(n < LAYERS)
        def _():
            wait_bytes(bcuo.at[n, pl.ds(0, 3)], ys.at[n, 0])
            wait_bytes(suo.at[n, pl.ds(0, 3)], ys.at[n, 1])
            wait_bytes(bmo.at[n, pl.ds(0, 3)], ys.at[n, 2])
            wait_bytes(cmo.at[n, pl.ds(0, 3)], ys.at[n, 4])

        wait_bytes(smo.at[n, pl.ds(0, 3)], ys.at[n, 3])
        wait_bytes(ubuf.at[n + 1], outs.at[n])
        wait_bytes(grecv.at[l, pl.ds(0, 3)], xs.at[l, 4])
        for half in range(2):
            wait_bytes(lout.at[l, half, pl.ds(0, 3)], xs.at[l, half])
            wait_bytes(eout.at[l, half, pl.ds(0, 3)], xs.at[l, 2 + half])
        for d in range(1, REACH + 1):

            @pl.when(z + d < nz)
            def _(d=d):
                wait_bytes(ggout.at[l], zs.at[l, 2, d - 1])
                for half in range(2):
                    wait_bytes(tout.at[l, half], zs.at[l, half, d - 1])

        @pl.when(seg < nseg - 1)
        def _():
            wait_bytes(halo.at[l], hs.at[l])

        @pl.when(relays(n))
        def _():
            wait_bytes(wbuf.at[l], wrs.at[n])
            for i, rows in enumerate((WPART, WPART, WHALF, WPART - WHALF)):
                wait_bytes(piece(n, x, 0, rows), wxs.at[n, i])

        @pl.when(phase != l)
        def _():
            wait_bytes(ubuf.at[0], outr.at[l])
            wait_bytes(ppb.at[l], ppsem.at[l])

        return carry

    lax.fori_loop(0, LAYERS, drain, 0)

    @pl.when(phase > 0)
    def _():
        for dy in range(1, NY):
            wait_bytes(piece(1, x, 0, WPART), wss.at[(y + dy) % NY])
        wait_bytes(wbuf.at[0], wss.at[y])

    @pl.when(phase == 0)
    def _():
        for p in range(1, NY * NC):
            wait_bytes(bcuo.at[0, 0], p0s.at[p, 0])
            wait_bytes(suo.at[0, 0], p0s.at[p, 1])

    @pl.when(seg < nseg - 1)
    def _():
        wait_bytes(idsrc, idsem.at[0])


def body(
    stream, doc_ids, in_proj, conv_weight, conv_bias, decay_log, step_bias, skip_gain, norm_gain
):
    nseg = lax.axis_size("seg")
    nz = nseg // NX

    vmem = pltpu.VMEM
    dma = pltpu.SemaphoreType.DMA
    n1 = LAYERS + 1
    return pl.pallas_call(
        functools.partial(kernel, nz),
        out_shape=jax.ShapeDtypeStruct((1, MICRO, T, CH * GROUPS), BF16),
        in_specs=[
            pl.BlockSpec(memory_space=pl.ANY),
            pl.BlockSpec(memory_space=pltpu.VMEM),
            pl.BlockSpec(memory_space=pl.ANY),
        ]
        + [pl.BlockSpec(memory_space=pltpu.VMEM)] * 6,
        out_specs=pl.BlockSpec(memory_space=pl.ANY),
        scratch_shapes=[
            vmem((LAYERS - 1, PROJ, CH), BF16),
            vmem((PROJ, CH * GROUPS), BF16),
            vmem((MICRO, T, CH * GROUPS), BF16),
            vmem((LAYERS + 2, T, CH), BF16),
            vmem((T, CH), F32),
            vmem((T, CH), BF16),
            vmem((GROUPS, 88, 128), F32),
            vmem((HEADS, 128), F32),
            vmem((PROJ, T), F32),
            vmem((LAYERS, 88, 128), F32),
            vmem((8, T), jnp.int32),
            vmem((8, T), jnp.int32),
            vmem((KERNEL, T, T), F32),
            vmem((LAYERS, 16, CH), BF16),
            vmem((T + 16, CH), F32),
            vmem((T, CH), BF16),
            vmem((NCH, T, 256), BF16),
            vmem((n1, NY, T, 128), BF16),
            vmem((n1, NY, 64, 128), BF16),
            vmem((n1, NY, 64, 128), BF16),
            vmem((n1, NY, T, 128), BF16),
            vmem((n1, NY, 64, 128), BF16),
            vmem((n1, NY, 64, 128), BF16),
            vmem((n1, NY, 16, 128), F32),
            vmem((n1, NY, 24, 128), F32),
            vmem((n1, NY, 16, 128), F32),
            vmem((n1, NY, 24, 128), F32),
            vmem((2, 16, 128), F32),
            vmem((LAYERS, 2, NX, 16, CH // 2), BF16),
            vmem((LAYERS, 2, NX, 16, CH // 2), BF16),
            vmem((LAYERS, 8, 128), F32),
            vmem((LAYERS, NX, 8, 128), F32),
            vmem((LAYERS, 2, 16, CH // 2), BF16),
            vmem((LAYERS, 8, 128), F32),
            vmem((LAYERS, 2, REACH, 16, CH // 2), BF16),
            vmem((LAYERS, REACH, 8, 128), F32),
            vmem((3, 16, CH), F32),
            vmem((LAYERS, 2, NX, 16, CH // 2), BF16),
            vmem((LAYERS, 2, NX, 16, CH // 2), BF16),
            vmem((T, CH), F32),
            vmem((T, CH), F32),
            dma((n1, 5)),
            dma((n1, 5)),
            dma((NY * NC, 2)),
            dma((LAYERS, 5)),
            dma((LAYERS, 5)),
            dma((LAYERS, 3, REACH)),
            dma((LAYERS, 3, REACH)),
            dma((LAYERS,)),
            dma((LAYERS,)),
            dma((LAYERS, 7)),
            dma((NY,)),
            dma((LAYERS,)),
            dma((LAYERS, 4)),
            dma((NY * NC,)),
            dma((NY * NC,)),
            dma((n1,)),
            dma((2,)),
            dma((4,)),
        ],
        compiler_params=pltpu.CompilerParams(
            collective_id=0, has_side_effects=True, vmem_limit_bytes=60 * 1024 * 1024
        ),
    )(
        stream,
        doc_ids,
        jnp.swapaxes(in_proj, 1, 2),
        conv_weight,
        conv_bias,
        decay_log,
        step_bias,
        skip_gain,
        norm_gain,
    )


def solution(mesh):
    placed = (
        P(None, "seg", None),
        P(None, "seg"),
        P("phase", None, None),
        P("phase", None, None),
        P("phase", None),
        P("phase", None),
        P("phase", None),
        P("phase", None),
        P("phase", None),
    )
    return jax.shard_map(
        body, mesh=mesh, in_specs=placed, out_specs=P("phase", None, "seg", None), check_vma=False
    )
```

```python
import functools

import jax
import jax.numpy as jnp
from jax import lax
from jax.experimental import pallas as pl
from jax.experimental.pallas import tpu as pltpu
from jax.sharding import PartitionSpec as P

NY = 4
NC = 2
NX = 4
LAYERS = 8
HEADS = 64
HEAD_DIM = 64
STATE = 64
GROUPS = 4
KERNEL = 4
MICRO = 2
T = 128
CH = 1024
PER = 16
NCH = 8
REACH = 4
PROJ = 576
WPART = 144
WHALF = 80
MESH = pl.DeviceIdType.MESH
F32 = jnp.float32
BF16 = jnp.bfloat16


def wait_bytes(ref, sem):
    pltpu.make_async_copy(ref, ref, sem).wait()


def kernel(
    nz,
    stream_ref,
    ids_ref,
    proj_ref,
    convw_ref,
    convb_ref,
    decay_ref,
    stepb_ref,
    skip_ref,
    norm_ref,
    out_ref,
    wbuf,
    w0,
    strm,
    ubuf,
    gm,
    gmb,
    pps,
    pph,
    p0,
    ppb,
    idsrc,
    idh,
    msk,
    halo,
    fbuf,
    inp,
    wts,
    bcu,
    bcm,
    bcuo,
    bcmo,
    su,
    sm,
    suo,
    smo,
    sg,
    lout,
    lrecv,
    gout,
    grecv,
    tout,
    ggout,
    trecv,
    ggrecv,
    rb,
    eout,
    ent,
    m0,
    gx,
    yr,
    ys,
    p0s,
    xr,
    xs,
    zr,
    zs,
    hr,
    hs,
    wr,
    wss,
    wrs,
    wxs,
    ppsem,
    outr,
    outs,
    idsem,
    loc,
):
    phase = lax.axis_index("phase")
    seg = lax.axis_index("seg")
    nseg = nz * NX
    y = phase // NC
    c = phase % NC
    z = seg // NX
    x = seg % NX

    def remote(src, dst, ssem, rsem, p, s):
        return pltpu.make_async_remote_copy(
            src_ref=src,
            dst_ref=dst,
            send_sem=ssem,
            recv_sem=rsem,
            device_id=(p, s),
            device_id_type=MESH,
        )

    barrier = pltpu.get_barrier_semaphore()
    count = 0
    for d in range(1, NY * NC):
        pl.semaphore_signal(barrier, inc=1, device_id=((phase + d) % (NY * NC), seg), device_id_type=MESH)
        count += 1
    for d in range(1, NX):
        pl.semaphore_signal(
            barrier, inc=1, device_id=(phase, z * NX + (x + d) % NX), device_id_type=MESH
        )
        count += 1
    for d in range(1, nz):
        pl.semaphore_signal(
            barrier, inc=1, device_id=(phase, ((z + d) % nz) * NX + x), device_id_type=MESH
        )
        count += 1
    for d in (1, nseg - 1):
        pl.semaphore_signal(barrier, inc=1, device_id=(phase, (seg + d) % nseg), device_id_type=MESH)
        count += 1

    cp_u = pltpu.make_async_copy(
        stream_ref.at[c, :, pl.ds(pl.multiple_of(y * CH, CH), CH)], ubuf.at[0], loc.at[0]
    )
    cp_u.start()
    def quarter(g):
        return proj_ref.at[0, :, pl.ds(pl.multiple_of(g * CH, CH), CH)]

    cp_w0 = pltpu.make_async_copy(proj_ref.at[0], w0, loc.at[1])
    cp_s0 = pltpu.make_async_copy(stream_ref, strm, loc.at[3])

    @pl.when(phase == 0)
    def _():
        cp_w0.start()
        cp_s0.start()

    @pl.when(phase > 0)
    def _():
        pltpu.make_async_copy(quarter(y), wbuf.at[phase - 1], loc.at[2]).start()

    low8 = lax.broadcasted_iota(jnp.int32, (8, 128), 1) < 64
    for g in range(GROUPS):
        for j in range(NCH):
            cj = pl.ds(CH * g + 128 * j, 128)
            for k in range(KERNEL):
                pps[g, pl.ds(8 * k + j, 1), :] = convw_ref[0, pl.ds(k, 1), cj]
            pps[g, pl.ds(32 + j, 1), :] = convb_ref[:, cj]
            pps[g, pl.ds(40 + j, 1), :] = norm_ref[:, cj]

    def per_head(ref):
        return jnp.transpose(jnp.broadcast_to(ref[...], (128, HEADS)))

    pph[...] = per_head(skip_ref)
    decay_rows = per_head(decay_ref)
    stepb_rows = per_head(stepb_ref)
    for g in range(GROUPS):
        pps[g, 48:56] = jnp.where(
            low8, pph[pl.ds(PER * g, 8, stride=2), :], pph[pl.ds(PER * g + 1, 8, stride=2), :]
        )
        pps[g, 56:72] = decay_rows[PER * g : PER * g + PER]
        pps[g, 72:88] = stepb_rows[PER * g : PER * g + PER]
    ppb[phase] = pps[y]

    pl.semaphore_wait(barrier, count)

    idsrc[...] = jnp.broadcast_to(ids_ref[pl.ds(c, 1), :], (8, T))

    @pl.when(seg < nseg - 1)
    def _():
        remote(idsrc, idh, idsem.at[0], idsem.at[1], phase, seg + 1).start()

    @pl.when(seg == 0)
    def _():
        idh[...] = jnp.full((8, T), -1, jnp.int32)

    def send_params():
        for d in range(1, NY * NC):
            p = (phase + d) % (NY * NC)
            remote(pps.at[p // NC], ppb.at[phase], ppsem.at[p], wr.at[phase, 6], p, seg).start()

    def part(n, i, r0, rows):
        return wbuf.at[n - 1, pl.ds(pl.multiple_of(i * WPART + r0, 16), rows), :]

    def send_weights():
        rows = pl.ds(pl.multiple_of(x * WPART, 16), WPART)
        for dy in (2, 1, 3):
            yd = (y + dy) % NY
            remote(
                proj_ref.at[0, rows, pl.ds(pl.multiple_of(yd * CH, CH), CH)],
                part(phase, x, 0, WPART),
                wss.at[yd],
                wr.at[phase, 0],
                yd * NC + c,
                seg,
            ).start()
        remote(quarter(y), wbuf.at[phase - 1], wss.at[y], wr.at[phase, 5], y * NC + 1 - c, seg).start()

    def relays(n):
        return (n < LAYERS) & (c == n % NC) & (y != n // NC)

    right = z * NX + (x + 1) % NX
    left = z * NX + (x + NX - 1) % NX

    def weights_1(n):
        @pl.when(relays(n))
        def _():
            mine = part(n, x, 0, WPART)
            wait_bytes(mine, wr.at[n, 0])
            remote(mine, mine, wxs.at[n, 0], wr.at[n, 1], phase, right).start()
            remote(mine, mine, wxs.at[n, 1], wr.at[n, 2], phase, left).start()

    def weights_2(n):
        @pl.when(relays(n))
        def _():
            wait_bytes(part(n, x, 0, WPART), wr.at[n, 1])
            first = part(n, (x + NX - 1) % NX, 0, WHALF)
            remote(first, first, wxs.at[n, 2], wr.at[n, 3], phase, right).start()
            wait_bytes(part(n, x, 0, WPART), wr.at[n, 2])
            last = part(n, (x + 1) % NX, WHALF, WPART - WHALF)
            remote(last, last, wxs.at[n, 3], wr.at[n, 4], phase, left).start()

    def weights_3(n):
        @pl.when(relays(n))
        def _():
            wait_bytes(part(n, x, 0, WHALF), wr.at[n, 3])
            wait_bytes(part(n, x, 0, WPART - WHALF), wr.at[n, 4])
            whole = wbuf.at[n - 1]
            remote(whole, whole, wrs.at[n], wr.at[n, 5], y * NC + 1 - c, seg).start()

        @pl.when((n < LAYERS) & (c != n % NC))
        def _():
            wait_bytes(wbuf.at[n - 1], wr.at[n, 5])

    lane = lax.broadcasted_iota(jnp.int32, (T, 128), 1)
    low = lane < 64

    def product(w, a):
        return lax.dot_general(w, a, (((1,), (1,)), ((), ())), preferred_element_type=F32)

    def rows_of(a, g):
        return jnp.concatenate(
            [a[64 * g : 64 * g + 64], a[256 + 64 * g : 320 + 64 * g]], axis=0
        ).astype(BF16)

    @pl.when(phase == 0)
    def _():
        send_params()
        cp_w0.wait()
        cp_s0.wait()
        for m in range(MICRO):
            at = LAYERS * m
            mine = strm[m]
            for r in range(4):
                rr = pl.ds(WPART * r, WPART)
                p0[rr, :] = product(w0[rr, :], mine)
            for g in range(GROUPS):
                bcuo[at, g, 0:64] = p0[pl.ds(64 * g, 64), :].astype(BF16)
                bcuo[at, g, 64:128] = p0[pl.ds(256 + 64 * g, 64), :].astype(BF16)
                suo[at, g] = p0[pl.ds(512 + 16 * g, 16), :]
            for g in (2, 1, 3, 0):
                p = g * NC + m
                if p > 0:
                    remote(bcuo.at[at, g], bcu.at[0, 0], p0s.at[p, 0], yr.at[0, 0], p, seg).start()
                    remote(suo.at[at, g], su.at[0, 0], p0s.at[p, 1], yr.at[0, 1], p, seg).start()
        bcu[0, 0] = bcuo[0, 0]
        su[0, 0] = suo[0, 0]

    @pl.when(phase == 1)
    def _():
        send_weights()
        send_params()

    cp_u.wait()

    @pl.when(phase > 0)
    def _():
        pltpu.make_async_copy(quarter(y), wbuf.at[phase - 1], loc.at[2]).wait()

    bcm[0] = jnp.zeros((NY, T, 128), BF16)
    sm[0] = jnp.zeros((NY, 24, 128), F32)
    for s in range(1, NY):
        bcu[0, s] = jnp.zeros((T, 128), BF16)
        su[0, s] = jnp.zeros((16, 128), F32)
    gm[...] = jnp.zeros((T, CH), F32)

    @pl.when(seg > 0)
    def _():
        wait_bytes(idh, idsem.at[1])

    own_row = idsrc[...].astype(F32)
    prior_row = idh[...].astype(F32)
    lane8 = lax.broadcasted_iota(jnp.int32, (8, T), 1)
    row_rep = jnp.broadcast_to(own_row[0:1], (T, T))
    col_rep = jnp.transpose(row_rep)
    t_at = lax.broadcasted_iota(jnp.int32, (T, T), 0)
    msk[0] = jnp.where((row_rep == col_rep) & (t_at >= lane), 1.0, 0.0)
    for k in range(1, KERNEL):
        behind = jnp.where(lane8 < k, pltpu.roll(prior_row, k, 1), pltpu.roll(own_row, k, 1))
        same = jnp.where(behind == own_row, 1.0, 0.0)
        msk[k] = jnp.transpose(jnp.broadcast_to(same[0:1], (T, T)))
    prior_last = jnp.broadcast_to(prior_row[:, T - 1 : T], (8, T))
    own_last = jnp.broadcast_to(own_row[:, T - 1 : T], (8, T))
    sg[1, 0:8] = jnp.where(own_row == prior_last, 1.0, 0.0)
    sg[1, 8:16] = jnp.where(own_row == own_last, 1.0, 0.0)
    sum_up = jnp.where(t_at <= lane, 1.0, 0.0)

    def total_square(lx):
        s = sm[lx, 0, 16:24] + sm[lx, 1, 16:24] + sm[lx, 2, 16:24] + sm[lx, 3, 16:24]
        return lax.rsqrt(s * (1.0 / (CH * GROUPS)) + 1e-05)

    def new_tokens(lx, inv_rep):
        for j in range(NCH):
            cj = pl.ds(128 * j, 128)
            u = ubuf[lx, :, cj].astype(F32) + gm[:, cj] * inv_rep
            ub = u.astype(BF16)
            ubuf[lx + 1, :, cj] = ub
            fbuf[pl.ds(16, T), cj] = ub.astype(F32)

    def send_out(lx):
        there = out_ref.at[0, c, :, pl.ds(pl.multiple_of(y * CH, CH), CH)]

        @pl.when(phase == lx - 1)
        def _():
            pltpu.make_async_copy(ubuf.at[lx + 1], there, outs.at[lx]).start()

        @pl.when(phase != lx - 1)
        def _():
            remote(ubuf.at[lx + 1], there, outs.at[lx], outr.at[phase], lx - 1, seg).start()

    def wait_square(lx):
        wait_bytes(sm.at[lx, pl.ds(0, 3)], yr.at[lx, 3])

    def push(lx, kind, outbuf, inbuf):
        for dy in (2, 1, 3):
            yd = (y + dy) % NY
            remote(
                outbuf.at[lx, yd], inbuf.at[lx, y], ys.at[lx, kind], yr.at[lx, kind], yd * NC + c, seg
            ).start()
        inbuf[lx, y] = outbuf[lx, y]

    def conv_rows(l, r0, n):
        for j in range(NCH):
            cj = pl.ds(128 * j, 128)
            acc = fbuf[pl.ds(16 + r0, n), cj] * ppb[l, pl.ds(24 + j, 1), :] + ppb[l, pl.ds(32 + j, 1), :]
            for k in range(1, KERNEL):
                tap = ppb[l, pl.ds(8 * (3 - k) + j, 1), :]
                acc = acc + (fbuf[pl.ds(16 + r0 - k, n), cj] * msk[k, pl.ds(r0, n), :]) * tap
            inp[pl.ds(r0, n), cj] = (acc * (1.0 / (1.0 + jnp.exp(-acc)))).astype(BF16)

    def layer(l, carry):
        @pl.when((l == 0) & (phase > 0))
        def _():
            wait_bytes(su.at[0, 0], yr.at[0, 1])

        @pl.when(l > 0)
        def _():
            wait_bytes(su.at[l, pl.ds(0, 3)], yr.at[l, 1])
            wait_square(l)

        inv8 = total_square(l)
        inv_rep = jnp.transpose(jnp.broadcast_to(inv8[0:1], (T, T)))
        new_tokens(l, inv_rep)

        @pl.when(seg < nseg - 1)
        def _():
            remote(
                ubuf.at[l + 1, pl.ds(T - 16, 16), :], halo.at[l], hs.at[l], hr.at[l], phase, seg + 1
            ).start()

        @pl.when(l == 0)
        def _():
            weights_1(1)

        @pl.when(l > 0)
        def _():
            weights_2(l + 1)

        @pl.when((l == 0) & (phase == 2))
        def _():
            send_weights()
            send_params()

        @pl.when(phase != l)
        def _():
            wait_bytes(ppb.at[l], wr.at[l, 6])

        s_u = su[l, 0] + su[l, 1] + su[l, 2] + su[l, 3]
        s_m = sm[l, 0, 0:16] + sm[l, 1, 0:16] + sm[l, 2, 0:16] + sm[l, 3, 0:16]
        pre = s_u + inv8[0:1] * s_m + ppb[l, 72:88]
        step = jnp.maximum(pre, 0.0) + jnp.log1p(jnp.exp(-jnp.abs(pre)))
        log_decay = -jnp.exp(ppb[l, 56:72]) * step
        run = jnp.dot(log_decay, sum_up, preferred_element_type=F32, precision=lax.Precision.HIGHEST)
        goes_on = sg[1, 0:1]
        is_last = sg[1, 8:9]
        cgain = jnp.exp(run) * goes_on
        tail = jnp.exp(jnp.broadcast_to(run[:, T - 1 : T], (PER, T)) - run) * is_last * step
        sg[0] = jnp.broadcast_to(cgain[:, T - 1 : T], (PER, T))
        gain8 = jnp.where(
            lane8 < 64, sg[0, pl.ds(0, 8, stride=2), :], sg[0, pl.ds(1, 8, stride=2), :]
        )
        gout[l] = gain8
        grecv[l, x] = gain8
        for d in range(1, NX):
            xd = (x + d) % NX
            remote(gout.at[l], grecv.at[l, x], xs.at[l, 1], xr.at[l, 1], phase, z * NX + xd).start()

        conv_rows(l, 16, T - 16)

        @pl.when((l == 0) & (phase > 0))
        def _():
            wait_bytes(bcu.at[0, 0], yr.at[0, 0])

        @pl.when(l > 0)
        def _():
            wait_bytes(bcu.at[l, pl.ds(0, 3)], yr.at[l, 0])
            wait_bytes(bcm.at[l, pl.ds(0, 3)], yr.at[l, 2])

        bc_u = (
            bcu[l, 0].astype(F32) + bcu[l, 1].astype(F32) + bcu[l, 2].astype(F32) + bcu[l, 3].astype(F32)
        )
        bc_m = (
            bcm[l, 0].astype(F32) + bcm[l, 1].astype(F32) + bcm[l, 2].astype(F32) + bcm[l, 3].astype(F32)
        )
        bc = (bc_u + inv8[0:1] * bc_m).astype(BF16)
        bt = bc[0:64].astype(F32)
        cs = jnp.transpose(bc[64:128].astype(F32)).astype(BF16)
        scores = jnp.dot(cs, bc[0:64], preferred_element_type=F32)
        scores = scores * msk[0]

        @pl.when(seg > 0)
        def _():
            wait_bytes(halo.at[l], hr.at[l])

        @pl.when(seg == 0)
        def _():
            halo[l] = jnp.zeros((16, CH), BF16)

        fbuf[pl.ds(0, 16), :] = halo[l].astype(F32)
        conv_rows(l, 0, 16)

        low64 = low[0:64]
        for j in range(NCH):
            cj = pl.ds(128 * j, 128)
            left = jnp.concatenate([bt * tail[2 * j : 2 * j + 1], bt * tail[2 * j + 1 : 2 * j + 2]], axis=0)
            both = jnp.dot(left.astype(BF16), inp[:, cj], preferred_element_type=F32)
            st = jnp.where(low64, both[0:64], both[64:128]).astype(BF16)
            for q in range(NX):
                lout[l, q, :, cj] = st[16 * q : 16 * q + 16]
        for d in (2, 1, 3):
            xd = (x + d) % NX
            remote(
                lout.at[l, xd], lrecv.at[l, x], xs.at[l, 0], xr.at[l, 0], phase, z * NX + xd
            ).start()
        lrecv[l, x] = lout[l, x]

        @pl.when(l > 0)
        def _():
            send_out(l)

        @pl.when(l == 0)
        def _():
            weights_2(1)

        @pl.when(phase == l + 3)
        def _():
            send_weights()
            send_params()

        cols = jnp.transpose(jnp.concatenate([run, cgain, jnp.zeros((T - 2 * PER, T), F32)], axis=0))
        for j in range(NCH):
            for i in range(2):
                h = 2 * j + i
                gap = jnp.broadcast_to(cols[:, h : h + 1], (T, T)) - run[h : h + 1]
                w = scores * (jnp.exp(jnp.minimum(gap, 0.0)) * step[h : h + 1])
                wts[j, :, pl.ds(128 * i, 128)] = w.astype(BF16)

        for j in range(NCH):
            cj = pl.ds(128 * j, 128)
            v = inp[:, cj]
            vf = v.astype(F32)
            right = jnp.concatenate([jnp.where(low, vf, 0.0), jnp.where(low, 0.0, vf)], axis=0).astype(BF16)
            intra = jnp.dot(wts[j], right, preferred_element_type=F32)
            m0[:, cj] = intra + ppb[l, pl.ds(48 + j, 1), :] * vf

        wait_bytes(grecv.at[l, pl.ds(0, 3)], xr.at[l, 1])
        wait_bytes(lrecv.at[l, pl.ds(0, 3)], xr.at[l, 0])
        p1 = grecv[l, 0]
        p2 = p1 * grecv[l, 1]
        p3 = p2 * grecv[l, 2]
        ggout[l] = p3 * grecv[l, 3]
        ga = grecv[l, 1]
        gb = grecv[l, 2]
        gc = grecv[l, 3]
        for j in range(NCH):
            cj = pl.ds(128 * j, 128)
            r1 = lrecv[l, 0, :, cj].astype(F32)
            r2 = lrecv[l, 1, :, cj].astype(F32) + ga[j : j + 1] * r1
            r3 = lrecv[l, 2, :, cj].astype(F32) + gb[j : j + 1] * r2
            rt = lrecv[l, 3, :, cj].astype(F32) + gc[j : j + 1] * r3
            rb[0, :, cj] = r1
            rb[1, :, cj] = r2
            rb[2, :, cj] = r3
            tout[l, :, cj] = rt.astype(BF16)
        for d in range(1, REACH + 1):

            @pl.when(z + d < nz)
            def _(d=d):
                to = (z + d) * NX + x
                remote(
                    ggout.at[l], ggrecv.at[l, d - 1], zs.at[l, REACH + d - 1], zr.at[l, REACH + d - 1], phase, to
                ).start()
                remote(tout.at[l], trecv.at[l, d - 1], zs.at[l, d - 1], zr.at[l, d - 1], phase, to).start()

        n = l + 1

        @pl.when(n < LAYERS)
        def _():
            weights_3(n)
            a = product(wbuf[l], ubuf[l + 1])
            for g in range(GROUPS):
                bcuo[n, g] = rows_of(a, g)
                suo[n, g] = a[512 + 16 * g : 528 + 16 * g]
            push(n, 1, suo, su)
            push(n, 0, bcuo, bcu)

        for d in range(1, REACH + 1):

            @pl.when(z >= d)
            def _(d=d):
                wait_bytes(ggrecv.at[l, d - 1], zr.at[l, REACH + d - 1])
                wait_bytes(trecv.at[l, d - 1], zr.at[l, d - 1])

            @pl.when(z < d)
            def _(d=d):
                ggrecv[l, d - 1] = jnp.zeros((8, 128), F32)
                trecv[l, d - 1] = jnp.zeros((16, CH), BF16)

        for j in range(NCH):
            cj = pl.ds(128 * j, 128)
            e = trecv[l, 3, :, cj].astype(F32)
            for d in (2, 1, 0):
                e = trecv[l, d, :, cj].astype(F32) + ggrecv[l, d, pl.ds(j, 1), :] * e
            eout[l, 0, :, cj] = e.astype(BF16)
            eout[l, 1, :, cj] = (rb[0, :, cj] + p1[j : j + 1] * e).astype(BF16)
            eout[l, 2, :, cj] = (rb[1, :, cj] + p2[j : j + 1] * e).astype(BF16)
            eout[l, 3, :, cj] = (rb[2, :, cj] + p3[j : j + 1] * e).astype(BF16)
        for d in (2, 1, 3):
            xd = (x + d) % NX
            remote(
                eout.at[l, xd], ent.at[l, x], xs.at[l, 2], xr.at[l, 2], phase, z * NX + xd
            ).start()
        ent[l, x] = eout[l, x]

        for j in range(NCH):
            g0 = jnp.broadcast_to(cols[:, PER + 2 * j : PER + 2 * j + 1], (T, T))
            g1 = jnp.broadcast_to(cols[:, PER + 2 * j + 1 : PER + 2 * j + 2], (T, T))
            gx[:, pl.ds(128 * j, 128)] = jnp.where(low, g0, g1)
        wait_bytes(ent.at[l, pl.ds(0, 3)], xr.at[l, 2])
        weights_1(n + 1)
        sq = jnp.zeros((T, 128), F32)
        for j in range(NCH):
            cj = pl.ds(128 * j, 128)
            part = jnp.dot(cs, ent[l, :, :, cj].reshape(STATE, 128), preferred_element_type=F32)
            mixed = m0[:, cj] + part * gx[:, cj]
            sq = sq + mixed * mixed
            scaled = ppb[l, pl.ds(40 + j, 1), :] * mixed
            gm[:, cj] = scaled
            gmb[:, cj] = scaled.astype(BF16)
        sq_row = jnp.broadcast_to(jnp.sum(jnp.transpose(sq), axis=0, keepdims=True), (8, T))
        for g in range(GROUPS):
            smo[n, g, 16:24] = sq_row

        @pl.when(n < LAYERS)
        def _():
            v = gmb[...]
            a = product(wbuf[l, 512:576, :], v)
            for g in range(GROUPS):
                smo[n, g, 0:16] = a[16 * g : 16 * g + 16]
            push(n, 3, smo, sm)
            a = product(wbuf[l, 0:512, :], v)
            for g in range(GROUPS):
                bcmo[n, g] = rows_of(a, g)
            push(n, 2, bcmo, bcm)

        @pl.when(n == LAYERS)
        def _():
            for g in range(GROUPS):
                smo[n, g, 0:16] = jnp.zeros((16, 128), F32)
            push(n, 3, smo, sm)

        return carry

    lax.fori_loop(0, LAYERS, layer, 0)

    wait_square(LAYERS)
    inv8 = total_square(LAYERS)
    new_tokens(LAYERS, jnp.transpose(jnp.broadcast_to(inv8[0:1], (T, T))))
    send_out(LAYERS)

    def drain(l, carry):
        n = l + 1

        @pl.when(n < LAYERS)
        def _():
            wait_bytes(bcuo.at[n, pl.ds(0, 3)], ys.at[n, 0])
            wait_bytes(suo.at[n, pl.ds(0, 3)], ys.at[n, 1])
            wait_bytes(bcmo.at[n, pl.ds(0, 3)], ys.at[n, 2])

        wait_bytes(smo.at[n, pl.ds(0, 3)], ys.at[n, 3])
        wait_bytes(ubuf.at[n + 1], outs.at[n])
        wait_bytes(lout.at[l, pl.ds(0, 3)], xs.at[l, 0])
        wait_bytes(grecv.at[l, pl.ds(0, 3)], xs.at[l, 1])
        wait_bytes(eout.at[l, pl.ds(0, 3)], xs.at[l, 2])
        for d in range(1, REACH + 1):

            @pl.when(z + d < nz)
            def _(d=d):
                wait_bytes(ggout.at[l], zs.at[l, REACH + d - 1])
                wait_bytes(tout.at[l], zs.at[l, d - 1])

        @pl.when(seg < nseg - 1)
        def _():
            wait_bytes(halo.at[l], hs.at[l])

        @pl.when(relays(n))
        def _():
            wait_bytes(wbuf.at[l], wrs.at[n])
            for i, rows in enumerate((WPART, WPART, WHALF, WPART - WHALF)):
                wait_bytes(part(n, x, 0, rows), wxs.at[n, i])

        @pl.when(phase != l)
        def _():
            wait_bytes(ubuf.at[0], outr.at[l])
            wait_bytes(ppb.at[l], ppsem.at[l])

        return carry

    lax.fori_loop(0, LAYERS, drain, 0)

    @pl.when(phase > 0)
    def _():
        for dy in range(1, NY):
            wait_bytes(part(1, x, 0, WPART), wss.at[(y + dy) % NY])
        wait_bytes(wbuf.at[0], wss.at[y])

    @pl.when(phase == 0)
    def _():
        for p in range(1, NY * NC):
            wait_bytes(bcuo.at[0, 0], p0s.at[p, 0])
            wait_bytes(suo.at[0, 0], p0s.at[p, 1])

    @pl.when(seg < nseg - 1)
    def _():
        wait_bytes(idsrc, idsem.at[0])


def body(
    stream, doc_ids, in_proj, conv_weight, conv_bias, decay_log, step_bias, skip_gain, norm_gain
):
    nseg = lax.axis_size("seg")
    nz = nseg // NX

    vmem = pltpu.VMEM
    dma = pltpu.SemaphoreType.DMA
    n1 = LAYERS + 1
    return pl.pallas_call(
        functools.partial(kernel, nz),
        out_shape=jax.ShapeDtypeStruct((1, MICRO, T, CH * GROUPS), BF16),
        in_specs=[
            pl.BlockSpec(memory_space=pl.ANY),
            pl.BlockSpec(memory_space=pltpu.VMEM),
            pl.BlockSpec(memory_space=pl.ANY),
        ]
        + [pl.BlockSpec(memory_space=pltpu.VMEM)] * 6,
        out_specs=pl.BlockSpec(memory_space=pl.ANY),
        scratch_shapes=[
            vmem((LAYERS - 1, PROJ, CH), BF16),
            vmem((PROJ, CH * GROUPS), BF16),
            vmem((MICRO, T, CH * GROUPS), BF16),
            vmem((LAYERS + 2, T, CH), BF16),
            vmem((T, CH), F32),
            vmem((T, CH), BF16),
            vmem((GROUPS, 88, 128), F32),
            vmem((HEADS, 128), F32),
            vmem((PROJ, T), F32),
            vmem((LAYERS, 88, 128), F32),
            vmem((8, T), jnp.int32),
            vmem((8, T), jnp.int32),
            vmem((KERNEL, T, T), F32),
            vmem((LAYERS, 16, CH), BF16),
            vmem((T + 16, CH), F32),
            vmem((T, CH), BF16),
            vmem((NCH, T, 256), BF16),
            vmem((n1, NY, T, 128), BF16),
            vmem((n1, NY, T, 128), BF16),
            vmem((n1, NY, T, 128), BF16),
            vmem((n1, NY, T, 128), BF16),
            vmem((n1, NY, 16, 128), F32),
            vmem((n1, NY, 24, 128), F32),
            vmem((n1, NY, 16, 128), F32),
            vmem((n1, NY, 24, 128), F32),
            vmem((2, 16, 128), F32),
            vmem((LAYERS, NX, 16, CH), BF16),
            vmem((LAYERS, NX, 16, CH), BF16),
            vmem((LAYERS, 8, 128), F32),
            vmem((LAYERS, NX, 8, 128), F32),
            vmem((LAYERS, 16, CH), BF16),
            vmem((LAYERS, 8, 128), F32),
            vmem((LAYERS, REACH, 16, CH), BF16),
            vmem((LAYERS, REACH, 8, 128), F32),
            vmem((3, 16, CH), F32),
            vmem((LAYERS, NX, 16, CH), BF16),
            vmem((LAYERS, NX, 16, CH), BF16),
            vmem((T, CH), F32),
            vmem((T, CH), F32),
            dma((n1, 4)),
            dma((n1, 4)),
            dma((NY * NC, 2)),
            dma((LAYERS, 3)),
            dma((LAYERS, 3)),
            dma((LAYERS, 2 * REACH)),
            dma((LAYERS, 2 * REACH)),
            dma((LAYERS,)),
            dma((LAYERS,)),
            dma((LAYERS, 7)),
            dma((NY,)),
            dma((LAYERS,)),
            dma((LAYERS, 4)),
            dma((NY * NC,)),
            dma((NY * NC,)),
            dma((n1,)),
            dma((2,)),
            dma((4,)),
        ],
        compiler_params=pltpu.CompilerParams(
            collective_id=0, has_side_effects=True, vmem_limit_bytes=60 * 1024 * 1024
        ),
    )(
        stream,
        doc_ids,
        jnp.swapaxes(in_proj, 1, 2),
        conv_weight,
        conv_bias,
        decay_log,
        step_bias,
        skip_gain,
        norm_gain,
    )


def solution(mesh):
    placed = (
        P(None, "seg", None),
        P(None, "seg"),
        P("phase", None, None),
        P("phase", None, None),
        P("phase", None),
        P("phase", None),
        P("phase", None),
        P("phase", None),
        P("phase", None),
    )
    return jax.shard_map(
        body, mesh=mesh, in_specs=placed, out_specs=P("phase", None, "seg", None), check_vma=False
    )
```
